32 devices in a mesh: group: 4 (over y, x), tile: 4 (over z), sub: 2 (over core).
Axes of the slice: x: 2, y: 2, z: 4, core: 2. Of those that a mesh axis runs over, the one named last changes fastest.
Arguments:
- substrate: float32 [128, 32, 1024], P('group', 'tile', 'sub'), may hold values from 0 to 1
- catalyst: float32 [128, 32, 1024], P('group', 'tile', 'sub'), may hold values from 0 to 1
- shear_offsets: int32 [2, 16], replicated, may hold values from 0 to 127
- slab_order: int32 [2, 4], replicated, may hold values from 0 to 3, each once within a row
- transfer_table: float32 [2, 2, 8], replicated, may hold values from 0.5 to 3.5
Outputs:
- substrate_out: float32 [128, 32, 1024], P('group', 'tile', 'sub')
- catalyst_out: float32 [128, 32, 1024], P('group', 'tile', 'sub')
- images: float32 [2, 32, 2048], P(None, 'tile', 'sub')
The draws below stay inside these ranges and needn't reach their ends.
Inputs may be any that keep to these rules, and one draw needn't show every extreme that they name: `slab_order`: each row is a permutation of 0 to 3.
All inputs are finite; a program needn't handle non-finite values.
Results may differ from the reference program's by a relative error of at most 0.0003.
Values may be sent and summed in bfloat16 or wider, within the bound.
A program may use at most 64 MiB of HBM per device.

```python
import jax
import jax.numpy as jnp
from jax import lax

CX = 32
STEPS = 2
VIEWS = 2
LEVELS = 8
SHEET = 8
NX = 128
NY = 32
NZ = 1024
SLABS = 4
OFFMAX = 128


def set_ends(entries, rng, low, high):
    longest = entries.shape.index(max(entries.shape))
    spots = []
    for shift in (0, 1):
        where = [jax.random.randint(jax.random.fold_in(rng, axis), (), 0, length) for axis, length in enumerate(entries.shape)]
        where[longest] = (where[longest] + shift) % entries.shape[longest]
        spots.append(tuple(where))
    return entries.at[spots[0]].set(low).at[spots[1]].set(high)


def shard_levels(rng, shape, split, smallest, high):
    def one(axis_at, blocks):
        heights = jax.random.uniform(jax.random.fold_in(jax.random.fold_in(rng, 6), axis_at), (blocks,), jnp.float32, smallest / len(split), high / len(split))
        return jnp.repeat(jnp.exp(heights), shape[axis_at] // blocks).reshape((-1,) + (1,) * (len(shape) - axis_at - 1))

    loudness = one(*split[0])
    for cut in split[1:]:
        loudness = loudness * one(*cut)
    return loudness


def setup_inputs(seed: int = 0) -> dict:
    streams_of = jax.random.split(jax.random.key(seed), 6)
    substrate = jnp.clip(1.0 * jax.random.uniform(streams_of[0], (NX, NY, NZ), jnp.float32) ** shard_levels(streams_of[0], (NX, NY, NZ), ((0, 4), (1, 4), (2, 2)), -0.2, 0.2), 0.0, 1.0)
    catalyst = jnp.clip(1.0 * jax.random.uniform(streams_of[1], (NX, NY, NZ), jnp.float32) ** shard_levels(streams_of[1], (NX, NY, NZ), ((0, 4), (1, 4), (2, 2)), -0.2, 0.2), 0.0, 1.0)
    shear_offsets = set_ends(jax.random.randint(streams_of[2], (VIEWS, NX // SHEET), 0, OFFMAX), jax.random.fold_in(streams_of[2], 1), 0, OFFMAX - 1).astype(jnp.int32)
    slab_order = jax.vmap(lambda own: jax.random.permutation(own, SLABS))(jax.random.split(streams_of[3], VIEWS)).reshape((VIEWS, SLABS)).astype(jnp.int32)
    transfer_table = jnp.clip(jax.random.uniform(streams_of[4], (VIEWS, 2, LEVELS), jnp.float32, 0.5, 3.5), 0.5, 3.5)
    return {"substrate": substrate, "catalyst": catalyst, "shear_offsets": shear_offsets, "slab_order": slab_order, "transfer_table": transfer_table}


SPREAD_FAST = 0.16
SPREAD_SLOW = 0.08
FEED_RATE = 0.04
KILL_RATE = 0.06
TIME_STEP = 1.0


def laplace(field):
    beside_all = jnp.roll(field, 1, 0) + jnp.roll(field, -1, 0)
    beside_all = beside_all + jnp.roll(field, 1, 1) + jnp.roll(field, -1, 1)
    beside_all = beside_all + jnp.roll(field, 1, 2) + jnp.roll(field, -1, 2)
    return beside_all - 6.0 * field


def lookup(levels, table_row):
    summed = jnp.zeros_like(levels)
    for level_index in range(LEVELS):
        summed = summed + table_row[level_index] * jnp.maximum(0.0, 1.0 - jnp.abs(levels - level_index))
    return summed


def render(scalar, offsets, table_pair, forward, ranks):
    depth_count = scalar.shape[0]
    height = scalar.shape[1]
    length = scalar.shape[2]
    margin = OFFMAX
    slab_count = depth_count // CX
    ascending = jnp.arange(CX, dtype=jnp.int32)
    local_order = jnp.where(forward, ascending, CX - 1 - ascending).astype(jnp.int32)

    def render_slab(slab_index):
        def visit_plane(state_pair, local_index):
            picture, before = state_pair
            plane_index = (slab_index * CX + local_index).astype(jnp.int32)
            current = lax.dynamic_index_in_dim(scalar, plane_index, 0, keepdims=False).astype(jnp.float32)
            following = jnp.concatenate([current[:, 1:], jnp.zeros((height, 1), jnp.float32)], axis=1)
            paired = jnp.stack([current, 0.5 * (current + following)], axis=-1).reshape(height, 2 * length)
            upsampled = jnp.concatenate([jnp.zeros((height, margin - 1), jnp.float32), 0.5 * current[:, :1], paired], axis=1)
            offset_now = lax.dynamic_index_in_dim(offsets, plane_index // SHEET, 0, keepdims=False).astype(jnp.int32)
            samples = lax.dynamic_slice(upsampled, (jnp.zeros((), jnp.int32), (margin - offset_now).astype(jnp.int32)), (height, 2 * length))
            levels = jnp.clip(samples, 0.0, 1.0) * (LEVELS - 1)
            extinction = lookup(levels, table_pair[0])
            emission = lookup(levels, table_pair[1])
            optical = extinction / depth_count
            picture = picture + emission * (-jnp.expm1(-optical)) * jnp.exp(-before)
            before = before + optical
            return (picture, before), None

        initial = jnp.zeros((height, 2 * length), jnp.float32)
        (picture, before), unused = lax.scan(visit_plane, (initial, initial), local_order)
        return picture, before

    colors, depths = lax.map(render_slab, jnp.arange(slab_count, dtype=jnp.int32))

    def add_slab(total, slab_index):
        own_rank = lax.dynamic_index_in_dim(ranks, slab_index, 0, keepdims=False)
        ahead = (ranks < own_rank).astype(jnp.float32)
        preceding = jnp.sum(ahead[:, None, None] * depths, axis=0)
        color = lax.dynamic_index_in_dim(colors, slab_index, 0, keepdims=False)
        return total + color * jnp.exp(-preceding), None

    picture, unused = lax.scan(add_slab, jnp.zeros((height, 2 * length), jnp.float32), jnp.arange(slab_count, dtype=jnp.int32))
    return picture


def reference(substrate, catalyst, shear_offsets, slab_order, transfer_table):
    for sweep_index in range(STEPS):
        lap_substrate = laplace(substrate)
        lap_catalyst = laplace(catalyst)
        reacting = substrate * catalyst * catalyst
        next_substrate = substrate + TIME_STEP * (SPREAD_FAST * lap_substrate - reacting + FEED_RATE * (1.0 - substrate))
        next_catalyst = catalyst + TIME_STEP * (SPREAD_SLOW * lap_catalyst + reacting - (FEED_RATE + KILL_RATE) * catalyst)
        substrate, catalyst = next_substrate, next_catalyst
    scalar = catalyst.astype(jnp.bfloat16)
    pictures = []
    for view_index in range(VIEWS):
        forward = slab_order[view_index, 1] > slab_order[view_index, 0]
        pictures.append(render(scalar, shear_offsets[view_index], transfer_table[view_index], forward, slab_order[view_index]))
    return substrate, catalyst, jnp.stack(pictures)
```

```python
import functools
import math

import jax
import jax.numpy as jnp
from jax import lax
from jax.experimental import pallas as pl
from jax.experimental.pallas import tpu as pltpu
from jax.sharding import PartitionSpec as P

LEVELS = 8
SHEET = 8
LANE = 128
LAG = 2

SPREAD_FAST = 0.16
SPREAD_SLOW = 0.08
FEED_RATE = 0.04
KILL_RATE = 0.06
TIME_STEP = 1.0

LOG2_E = math.log2(math.e)

CODE_TOP = 65535.0
TABLE_TOP = 3.5
CODE_SHIFT = 32768.0

MESH = pl.DeviceIdType.MESH


def encode(x, bound=1.0):
    return (jnp.round(x * (CODE_TOP / bound)) - CODE_SHIFT).astype(jnp.int32).astype(jnp.int16)


def decode(x, bound=1.0):
    return (x.astype(jnp.int32).astype(jnp.float32) + CODE_SHIFT) * (bound / CODE_TOP)


SPREADS = (TIME_STEP * SPREAD_FAST, TIME_STEP * SPREAD_SLOW)
KEEP_SUB = 1.0 - TIME_STEP * (6.0 * SPREAD_FAST + FEED_RATE)
KEEP_CAT = 1.0 - TIME_STEP * (6.0 * SPREAD_SLOW + FEED_RATE + KILL_RATE)


def react(sub, cat, beside_sub, beside_cat):
    reacting = TIME_STEP * (sub * cat * cat)
    new_sub = (SPREADS[0] * beside_sub + (TIME_STEP * FEED_RATE + KEEP_SUB * sub)) - reacting
    new_cat = (SPREADS[1] * beside_cat + KEEP_CAT * cat) + reacting
    return new_sub, new_cat


def kernel(
    counts,
    sub_in, cat_in, offsets, order, table,
    sub_out, cat_out, images,
    raw, mid, halo_send, halo_recv, halo, inner, mid_halo, edge_send, edge, scalar, bands, samples, slabs,
    load_sem, z_send, z_recv, x_send, x_recv, y_send, y_recv, d_send, d_recv,
    f_send, f_recv, g_send, g_recv,
):
    n_group, n_tile, n_sub = counts
    planes, rows, depth = sub_in.shape
    wide = depth + 2 * LANE
    own = pl.ds(LANE, depth)
    views = order.shape[0]
    sheets = planes // SHEET
    g, t, s = lax.axis_index("group"), lax.axis_index("tile"), lax.axis_index("sub")

    def at(dg=0, dt=0, ds=0):
        return (
            lax.rem(g + (dg + n_group), n_group),
            lax.rem(t + (dt + n_tile), n_tile),
            lax.rem(s + (ds + n_sub), n_sub),
        )

    barrier = pltpu.get_barrier_semaphore()
    peers = [at(ds=1), at(ds=-1), at(dt=1), at(dt=-1)]
    peers += [at(dg=a, dt=b) for a in (-1, 1) for b in (-1, 1)]
    peers += [at(dg=d) for d in range(1, n_group)]
    for peer in peers:
        pl.semaphore_signal(barrier, inc=1, device_id=peer, device_id_type=MESH)

    inputs = (sub_in, cat_in)
    loads = []
    for f in range(2):
        loads.append(
            pltpu.make_async_copy(inputs[f], raw.at[f, pl.ds(2, planes), :, own], load_sem.at[f])
        )
    for load in loads:
        load.start()

    def band_step(index, carry):
        k = index // sheets
        b = lax.rem(index, sheets)
        shift = offsets[k, g * sheets + b]
        depth_at = lax.broadcasted_iota(jnp.int32, (2 * LANE, 2 * LANE), 0)
        column = lax.broadcasted_iota(jnp.int32, (2 * LANE, 2 * LANE), 1)
        distance = (2 * depth_at - column) + (shift - LANE)
        weight = (LEVELS - 1) * jnp.maximum(0.0, 1.0 - 0.5 * jnp.abs(distance).astype(jnp.float32))
        bands[index] = weight.astype(jnp.bfloat16)
        return carry

    for load in loads:
        load.wait()

    outer = [(0, 0, rows - 2), (0, 1, rows - 1), (1, 0, 0), (1, 1, 1)]

    def collect(p, carry):
        for side, j, y in outer:
            for f in range(2):
                halo[side, f, j, pl.ds(p, 1), own] = raw[f, p + 2, y : y + 1, LANE : LANE + depth]
        return carry

    lax.fori_loop(0, planes, collect, 0, unroll=4)
    for side, j, y in outer:
        for f in range(2):
            halo_send[side, f, j] = encode(halo[side, f, j, :, LANE : LANE + depth])
    for a in range(2):
        for b in range(2):
            for f in range(2):
                plane = 2 + (planes - 1 if a == 0 else 0)
                row = rows - 1 if b == 0 else 0
                edge_send[a, b, f : f + 1] = raw[f, plane, row : row + 1, LANE : LANE + depth]

    pl.semaphore_wait(barrier, len(peers))

    def remote(src, dst, send, recv, to):
        return pltpu.make_async_remote_copy(
            src_ref=src, dst_ref=dst, send_sem=send, recv_sem=recv,
            device_id=to, device_id_type=MESH,
        )

    y_copies = [
        remote(halo_send.at[side], halo_recv.at[side, :, :, :, own],
               y_send.at[side], y_recv.at[side], at(dt=1 if side == 0 else -1))
        for side in range(2)
    ]
    d_copies = [
        remote(edge_send.at[a, b], edge.at[a, b, :, own], d_send.at[a, b], d_recv.at[a, b],
               at(dg=1 if a == 0 else -1, dt=1 if b == 0 else -1))
        for a in range(2) for b in range(2)
    ]
    x_copies = [
        remote(inputs[f].at[pl.ds(planes - 2 if a == 0 else 0, 2)],
               raw.at[f, pl.ds(0 if a == 0 else planes + 2, 2), :, own],
               x_send.at[a, f], x_recv.at[a, f], at(dg=1 if a == 0 else -1))
        for a in range(2) for f in range(2)
    ]
    z_copies = [
        remote(inputs[f].at[:, :, pl.ds(depth - LANE if a == 0 else 0, LANE)],
               raw.at[f, pl.ds(2, planes), :, pl.ds(0 if a == 0 else LANE + depth, LANE)],
               z_send.at[a, f], z_recv.at[a, f], at(ds=1 if a == 0 else -1))
        for a in range(2) for f in range(2)
    ]
    for copy in d_copies + y_copies + z_copies + x_copies:
        copy.start()

    lax.fori_loop(0, views * sheets, band_step, 0)

    row_of = lax.broadcasted_iota(jnp.int32, (rows, wide), 0)

    def along_z(x):
        return pltpu.roll(x, 1, 1) + pltpu.roll(x, wide - 1, 1)

    def along_y(x, low, high):
        below = jnp.where(row_of == 0, low, pltpu.roll(x, 1, 0))
        above = jnp.where(row_of == rows - 1, high, pltpu.roll(x, rows - 1, 0))
        return below + above

    def raw_plane(p, lows, highs):
        centers = [raw[f, p] for f in range(2)]
        besides = [
            raw[f, p + 1] + raw[f, p - 1]
            + along_y(centers[f], lows[f], highs[f]) + along_z(centers[f])
            for f in range(2)
        ]
        new = react(centers[0], centers[1], besides[0], besides[1])
        for f in range(2):
            mid[f, p - 1] = new[f]

    for copy in z_copies:
        copy.wait_recv()

    def first_step(p, carry):
        raw_plane(p + 2, (0.0, 0.0), (0.0, 0.0))
        for side in range(2):
            for f in range(2):
                row = 0 if side == 0 else rows - 1
                inner[side, f, pl.ds(p, 1)] = raw[f, p + 2, row : row + 1]
        return carry

    lax.fori_loop(1, planes - 1, first_step, 0, unroll=2)

    forwards = []

    def forward(view):
        for a in range(2):
            index = len(forwards)
            copy = remote(
                view(pl.ds(depth if a == 0 else LANE, LANE)),
                view(pl.ds(0 if a == 0 else LANE + depth, LANE)),
                f_send.at[index], f_recv.at[index], at(ds=1 if a == 0 else -1),
            )
            copy.start()
            forwards.append(copy)

    for index, copy in enumerate(x_copies):
        a, f = divmod(index, 2)
        copy.wait_recv()
        forward(lambda lanes: raw.at[f, pl.ds(0 if a == 0 else planes + 2, 2), :, lanes])
    for index, copy in enumerate(d_copies):
        a, b = divmod(index, 2)
        copy.wait_recv()
        forward(lambda lanes: edge.at[a, b, :, lanes])
    for copy in forwards:
        copy.wait_recv()
    arrived = len(forwards)
    for side, copy in enumerate(y_copies):
        copy.wait_recv()
        forward(lambda lanes: halo_recv.at[side, :, :, :, lanes])
    lax.fori_loop(0, 2, lambda i, carry: first_step(i * (planes - 1), carry), 0)
    for a, p in ((0, 1), (1, planes + 2)):
        ends = [
            [jnp.broadcast_to(edge[a, b, f : f + 1], (rows, wide)) for f in range(2)] for b in range(2)
        ]
        raw_plane(p, ends[0], ends[1])

    for copy in forwards[arrived:]:
        copy.wait_recv()

    for side in range(2):
        for f in range(2):
            for j in range(2):
                halo[side, f, j] = decode(halo_recv[side, f, j])

    def mend(p, carry):
        for side, j, y in ((0, 1, 0), (1, 0, rows - 1)):
            for f in range(2):
                mid[f, p + 1, y : y + 1] = (
                    mid[f, p + 1, y : y + 1] + SPREADS[f] * halo[side, f, j, pl.ds(p, 1)]
                )
        return carry

    lax.fori_loop(0, planes, mend, 0, unroll=4)

    plane_of = lax.broadcasted_iota(jnp.int32, (planes, wide), 0)
    for side in range(2):
        near, far = (1, 0) if side == 0 else (0, 1)
        centers, besides = [], []
        for f in range(2):
            center = halo[side, f, near]
            before = jnp.where(
                plane_of == 0, jnp.broadcast_to(edge[0, side, f : f + 1], center.shape),
                pltpu.roll(center, 1, 0),
            )
            after = jnp.where(
                plane_of == planes - 1, jnp.broadcast_to(edge[1, side, f : f + 1], center.shape),
                pltpu.roll(center, planes - 1, 0),
            )
            centers.append(center)
            besides.append(before + after + inner[side, f] + halo[side, f, far] + along_z(center))
        new = react(centers[0], centers[1], besides[0], besides[1])
        for f in range(2):
            mid_halo[side, f] = new[f]

    lane_of = lax.broadcasted_iota(jnp.int32, (rows, wide), 1)
    lowest = jnp.where(s == 0, LANE, 0)
    highest = jnp.where(s == n_sub - 1, LANE + depth, wide)
    inside = (lane_of >= lowest) & (lane_of < highest)

    def mid_plane(p):
        centers = [mid[f, p + 1] for f in range(2)]
        besides = [
            mid[f, p + 2] + mid[f, p]
            + along_y(
                centers[f],
                jnp.broadcast_to(mid_halo[0, f, pl.ds(p, 1)], (rows, wide)),
                jnp.broadcast_to(mid_halo[1, f, pl.ds(p, 1)], (rows, wide)),
            )
            + along_z(centers[f])
            for f in range(2)
        ]
        new_sub, new_cat = react(centers[0], centers[1], besides[0], besides[1])
        sub_out[p] = new_sub[:, LANE : LANE + depth]
        cat_out[p] = new_cat[:, LANE : LANE + depth]
        kept = jnp.where(inside, new_cat, 0.0)
        return pltpu.roll(kept, wide - LANE // 2, 1)[:, : wide - LANE]

    def second_step(pair, carry):
        both = jnp.concatenate([mid_plane(2 * pair), mid_plane(2 * pair + 1)], axis=0)
        scalar[pl.ds(pl.multiple_of(pair * 2 * rows, 2 * rows), 2 * rows)] = both.astype(jnp.bfloat16)
        return carry

    lax.fori_loop(0, planes // 2, second_step, 0, unroll=2)

    depth_total = float(planes * n_group)
    width = 2 * depth
    span = min(4 * LANE, width)
    parts = width // span
    dim_top = 1.00001 * -math.expm1(-planes * TABLE_TOP / depth_total)
    light_top = TABLE_TOP * dim_top
    g_copies = []
    chunks = [(k, part) for k in range(views) for part in range(parts)]

    def finish(k, part):
        for d in range(1, n_group):
            slot = slabs.at[at(dg=-d)[0], k, part]
            remote(slot, slot, g_send.at[d - 1, k, part], g_recv.at[d - 1, k, part],
                   at(dg=d)).wait_recv()
        total = jnp.zeros((rows, span), jnp.float32)
        coded = [slabs[slab, k, part] for slab in range(n_group)]
        lights = [decode(one[:rows], light_top) for one in coded]
        clears = [1.0 - decode(one[rows:], dim_top) for one in coded]
        for slab in range(n_group):
            passed = lights[slab]
            for other in range(n_group):
                if other != slab:
                    ahead = order[k, other] < order[k, slab]
                    passed = passed * jnp.where(ahead, clears[other], 1.0)
            total = total + passed
        images[k, :, part * span : (part + 1) * span] = total

    for k in range(views):
        def resample(b, carry):
            band = bands[k * sheets + b]
            size = SHEET * rows
            for c in range(depth // LANE):
                piece = scalar[pl.ds(pl.multiple_of(b * size, size), size), c * LANE : (c + 2) * LANE]
                out = jnp.dot(piece, band, preferred_element_type=jnp.float32)
                samples[pl.ds(b * SHEET, SHEET), :, 2 * c * LANE : 2 * (c + 1) * LANE] = out.reshape(
                    SHEET, rows, 2 * LANE
                )
            return carry

        lax.fori_loop(0, sheets, resample, 0)

        level_of = lax.broadcasted_iota(jnp.int32, (LEVELS, LANE), 0)
        lines = []
        for which, scale in ((0, -LOG2_E / depth_total), (1, 1.0)):
            values = [table[k, which, l] * scale for l in range(LEVELS)]
            intercepts = jnp.full((LEVELS, LANE), values[LEVELS - 1], jnp.float32)
            slopes = jnp.zeros((LEVELS, LANE), jnp.float32)
            for l in range(LEVELS - 1):
                slope = values[l + 1] - values[l]
                slopes = jnp.where(level_of == l, slope, slopes)
                intercepts = jnp.where(level_of == l, values[l] - l * slope, intercepts)
            lines += [intercepts, slopes]
        ascending = order[k, 1] > order[k, 0]

        def line(which, level, q):
            picked = [
                jnp.take_along_axis(values, level, axis=0, mode="promise_in_bounds")
                for values in lines[2 * which : 2 * which + 2]
            ]
            return picked[0] + picked[1] * q

        for part in range(parts):
            starts = [part * span + i * LANE for i in range(span // LANE)]

            def visit(i, state):
                p = jnp.where(ascending, i, planes - 1 - i)
                after = []
                for start, (light, depth_log, clear) in zip(starts, state):
                    q = jnp.clip(samples[p, :, start : start + LANE], 0.0, LEVELS - 1.0)
                    level = q.astype(jnp.int32)
                    depth_log = depth_log + line(0, level, q)
                    left = jnp.exp2(depth_log)
                    after.append((light + line(1, level, q) * (clear - left), depth_log, left))
                return tuple(after)

            none = jnp.zeros((rows, LANE), jnp.float32)
            state = lax.fori_loop(
                0, planes, visit, tuple((none, none, none + 1.0) for start in starts), unroll=8
            )
            for i, (light, _, clear) in enumerate(state):
                lanes = slice(i * LANE, (i + 1) * LANE)
                slabs[g, k, part, :, lanes] = jnp.concatenate(
                    [encode(light, light_top), encode(1.0 - clear, dim_top)], axis=0
                )
            for d in range(1, n_group):
                slot = slabs.at[g, k, part]
                copy = remote(slot, slot, g_send.at[d - 1, k, part], g_recv.at[d - 1, k, part], at(dg=d))
                copy.start()
                g_copies.append(copy)
            done = chunks.index((k, part)) - LAG
            if done >= 0:
                finish(*chunks[done])

    for chunk in chunks[-LAG:]:
        finish(*chunk)

    for copy in y_copies + d_copies + x_copies + z_copies + forwards:
        copy.wait_send()
    for copy in g_copies:
        copy.wait_send()


PIECES = 4


def hand_over(*refs):
    sources, targets, (sem,) = refs[:3], refs[3:6], refs[6:]
    copies = [pltpu.make_async_copy(a, b, sem.at[i]) for i, (a, b) in enumerate(zip(sources, targets))]
    for copy in copies:
        copy.start()
    for copy in copies:
        copy.wait()


def solution(mesh):
    counts = (mesh.shape["group"], mesh.shape["tile"], mesh.shape["sub"])

    def local(substrate, catalyst, shear_offsets, slab_order, transfer_table):
        planes, rows, depth = substrate.shape
        views = slab_order.shape[0]
        wide = depth + 2 * LANE
        sheets = planes // SHEET
        f32 = jnp.float32
        dma = pltpu.SemaphoreType.DMA
        smem = pl.BlockSpec(memory_space=pltpu.SMEM)
        vmem = pl.BlockSpec(memory_space=pltpu.VMEM)
        hbm = pl.BlockSpec(memory_space=pltpu.HBM)
        anywhere = pl.BlockSpec(memory_space=pl.ANY)
        width = 2 * depth
        span = min(4 * LANE, width)
        parts = width // span
        results = pl.pallas_call(
            functools.partial(kernel, counts),
            out_shape=(
                pltpu.VMEM(substrate.shape, f32),
                pltpu.VMEM(substrate.shape, f32),
                pltpu.VMEM((views, rows, 2 * depth), f32),
            ),
            in_specs=[hbm, hbm, smem, smem, smem],
            out_specs=(vmem, vmem, vmem),
            scratch_shapes=[
                pltpu.VMEM((2, planes + 4, rows, wide), f32),
                pltpu.VMEM((2, planes + 2, rows, wide), f32),
                pltpu.VMEM((2, 2, 2, planes, depth), jnp.int16),
                pltpu.VMEM((2, 2, 2, planes, wide), jnp.int16),
                pltpu.VMEM((2, 2, 2, planes, wide), f32),
                pltpu.VMEM((2, 2, planes, wide), f32),
                pltpu.VMEM((2, 2, planes, wide), f32),
                pltpu.VMEM((2, 2, 2, depth), f32),
                pltpu.VMEM((2, 2, 2, wide), f32),
                pltpu.VMEM((planes * rows, wide - LANE), jnp.bfloat16),
                pltpu.VMEM((views * sheets, 2 * LANE, 2 * LANE), jnp.bfloat16),
                pltpu.VMEM((planes, rows, 2 * depth), f32),
                pltpu.VMEM((counts[0], views, parts, 2 * rows, span), jnp.int16),
                dma((2,)), dma((2, 2)), dma((2, 2)), dma((2, 2)), dma((2, 2)),
                dma((2,)), dma((2,)), dma((2, 2)), dma((2, 2)),
                dma((20,)), dma((20,)),
                dma((counts[0] - 1, views, parts)), dma((counts[0] - 1, views, parts)),
            ],
            compiler_params=pltpu.CompilerParams(collective_id=0, has_side_effects=True, vmem_limit_bytes=60 * 2**20),
        )(substrate, catalyst, shear_offsets, slab_order, transfer_table)
        return pl.pallas_call(
            hand_over,
            out_shape=tuple(jax.ShapeDtypeStruct(one.shape, one.dtype) for one in results),
            in_specs=[vmem] * 3,
            out_specs=(anywhere,) * 3,
            scratch_shapes=[dma((3,))],
            compiler_params=pltpu.CompilerParams(vmem_limit_bytes=4 * 2**20),
        )(*results)

    placed = (P("group", "tile", "sub"), P("group", "tile", "sub"), P(), P(), P())
    return jax.shard_map(
        local,
        mesh=mesh,
        in_specs=placed,
        out_specs=(P("group", "tile", "sub"), P("group", "tile", "sub"), P(None, "tile", "sub")),
        check_vma=False,
    )
```

```python
import functools
import math

import jax
import jax.numpy as jnp
from jax import lax
from jax.experimental import pallas as pl
from jax.experimental.pallas import tpu as pltpu
from jax.sharding import PartitionSpec as P

LEVELS = 8
SHEET = 8
LANE = 128
SEAM = 32
TAKE_AT = 0

SPREAD_FAST = 0.16
SPREAD_SLOW = 0.08
FEED_RATE = 0.04
KILL_RATE = 0.06
TIME_STEP = 1.0

LOG2_E = math.log2(math.e)

CODE_TOP = 65535.0
TABLE_TOP = 3.5
CODE_SHIFT = 32768.0

MESH = pl.DeviceIdType.MESH


def encode(x, bound=1.0):
    return (jnp.round(x * (CODE_TOP / bound)) - CODE_SHIFT).astype(jnp.int32).astype(jnp.int16)


def decode(x, bound=1.0):
    return (x.astype(jnp.int32).astype(jnp.float32) + CODE_SHIFT) * (bound / CODE_TOP)


SPREADS = (TIME_STEP * SPREAD_FAST, TIME_STEP * SPREAD_SLOW)
KEEP_SUB = 1.0 - TIME_STEP * (6.0 * SPREAD_FAST + FEED_RATE)
KEEP_CAT = 1.0 - TIME_STEP * (6.0 * SPREAD_SLOW + FEED_RATE + KILL_RATE)


def react(sub, cat, beside_sub, beside_cat):
    reacting = TIME_STEP * (sub * cat * cat)
    new_sub = (SPREADS[0] * beside_sub + (TIME_STEP * FEED_RATE + KEEP_SUB * sub)) - reacting
    new_cat = (SPREADS[1] * beside_cat + KEEP_CAT * cat) + reacting
    return new_sub, new_cat


def kernel(
    counts,
    sub_in, cat_in, offsets, order, table,
    sub_out, cat_out, images,
    raw, mid, halo_send, halo_recv, halo, inner, outer, second, mid_edge, late, wide_cat,
    z_out, x_out, y_out, edge_send, edge, edge_out, scalars, bands, samples, slabs,
    load_sem, z_send, z_recv, x_send, x_recv, xf_send, xf_recv, y_send, y_recv, yf_send, yf_recv,
    d_send, d_recv, df_send, df_recv, g_send, g_recv,
):
    n_group, n_tile, n_sub = counts
    planes, rows, depth = sub_in.shape
    wide = depth + LANE
    own = pl.ds(LANE, depth)
    views = order.shape[0]
    sheets = planes // SHEET
    half = depth // 2
    last = rows - 1
    g, t, s = lax.axis_index("group"), lax.axis_index("tile"), lax.axis_index("sub")

    def at(dg=0, dt=0, ds=0):
        return (
            lax.rem(g + (dg + n_group), n_group),
            lax.rem(t + (dt + n_tile), n_tile),
            lax.rem(s + (ds + n_sub), n_sub),
        )

    partner = at(ds=1)

    barrier = pltpu.get_barrier_semaphore()
    peers = [partner, at(dt=1), at(dt=-1)]
    peers += [at(dg=a, dt=b) for a in (-1, 1) for b in (-1, 1)]
    peers += [at(dg=d) for d in range(1, n_group)]
    for peer in peers:
        pl.semaphore_signal(barrier, inc=1, device_id=peer, device_id_type=MESH)

    inputs = (sub_in, cat_in)
    loads = [
        pltpu.make_async_copy(inputs[f], raw.at[f, pl.ds(2, planes), :, own], load_sem.at[f])
        for f in range(2)
    ]
    for load in loads:
        load.start()

    def ring_block(low, high, lane_of):
        return jnp.where(lane_of < SEAM, low, high)

    lane_of = lax.broadcasted_iota(jnp.int32, (rows, LANE), 1)
    lane_of_planes = lax.broadcasted_iota(jnp.int32, (planes, LANE), 1)
    row_of = lax.broadcasted_iota(jnp.int32, (rows, wide), 0)
    first_block, last_block = slice(LANE, 2 * LANE), slice(depth, depth + LANE)
    ends = ((0, 1), (last, last - 1))

    def band_step(index, carry):
        k = index // sheets
        b = lax.rem(index, sheets)
        shift = offsets[k, g * sheets + b]
        depth_at = lax.broadcasted_iota(jnp.int32, (2 * LANE, 2 * LANE), 0)
        column = lax.broadcasted_iota(jnp.int32, (2 * LANE, 2 * LANE), 1)
        distance = (2 * depth_at - column) + (shift - LANE)
        weight = (LEVELS - 1) * jnp.maximum(0.0, 1.0 - 0.5 * jnp.abs(distance).astype(jnp.float32))
        bands[index] = weight.astype(jnp.bfloat16)
        return carry

    for load in loads:
        load.wait()

    def collect(p, carry):
        for f in range(2):
            z_out[f, p] = ring_block(raw[f, p + 2, :, first_block], raw[f, p + 2, :, last_block], lane_of)
        for side in range(2):
            near, far = ends[1 - side]
            for layer, (f, y) in enumerate(((0, near), (1, near), (1, far), (0, far))):
                halo[side, layer, pl.ds(p, 1), own] = raw[f, p + 2, y : y + 1, LANE:wide]
        return carry

    lax.fori_loop(0, planes, collect, 0, unroll=4)
    for side in range(2):
        for layer in range(4):
            halo_send[side, layer] = encode(halo[side, layer, :, LANE:wide])
    for a in range(2):
        for b in range(2):
            for f in range(2):
                plane = 2 + (planes - 1 if a == 0 else 0)
                row = last if b == 0 else 0
                edge_send[a, b, f : f + 1] = raw[f, plane, row : row + 1, LANE:wide]

    pl.semaphore_wait(barrier, len(peers))

    def remote(src, dst, send, recv, to):
        return pltpu.make_async_remote_copy(
            src_ref=src, dst_ref=dst, send_sem=send, recv_sem=recv,
            device_id=to, device_id_type=MESH,
        )

    y_copies = [
        [
            remote(halo_send.at[side, layers], halo_recv.at[side, layers, :, own],
                   y_send.at[part, side], y_recv.at[part, side], at(dt=1 if side == 0 else -1))
            for side in range(2)
        ]
        for part, layers in enumerate((pl.ds(0, 3), pl.ds(3, 1)))
    ]
    d_copies = [
        remote(edge_send.at[a, b], edge.at[a, b, :, own], d_send.at[a, b], d_recv.at[a, b],
               at(dg=1 if a == 0 else -1, dt=1 if b == 0 else -1))
        for a in range(2) for b in range(2)
    ]
    x_copies = [
        remote(inputs[f].at[pl.ds(planes - 2 if a == 0 else 0, 2)],
               raw.at[f, pl.ds(0 if a == 0 else planes + 2, 2), :, own],
               x_send.at[a, f], x_recv.at[a, f], at(dg=1 if a == 0 else -1))
        for a in range(2) for f in range(2)
    ]
    z_copies = [
        remote(z_out.at[f], raw.at[f, pl.ds(2, planes), :, pl.ds(0, LANE)], z_send.at[f], z_recv.at[f], partner)
        for f in range(2)
    ]
    started = d_copies + y_copies[0] + z_copies + x_copies + y_copies[1]
    for copy in started:
        copy.start()

    lax.fori_loop(0, views * sheets, band_step, 0)

    def along_z(x):
        return pltpu.roll(x, 1, 1) + pltpu.roll(x, wide - 1, 1)

    def along_y(x):
        below = jnp.where(row_of == 0, 0.0, pltpu.roll(x, 1, 0))
        above = jnp.where(row_of == last, 0.0, pltpu.roll(x, last, 0))
        return below + above

    def step(field, p):
        centers = [field[f, p] for f in range(2)]
        besides = [
            field[f, p + 1] + field[f, p - 1] + along_y(centers[f]) + along_z(centers[f]) for f in range(2)
        ]
        return react(centers[0], centers[1], besides[0], besides[1])

    def raw_plane(p):
        new = step(raw, p)
        for f in range(2):
            mid[f, p - 1] = new[f]

    def first_step(p, carry):
        raw_plane(p + 2)
        for side, (y, beside) in enumerate(ends):
            for f in range(2):
                inner[side, f, pl.ds(p, 1)] = raw[f, p + 2, y : y + 1]
                outer[side, f, pl.ds(p, 1)] = mid[f, p + 1, y : y + 1]
                second[side, f, pl.ds(p, 1)] = mid[f, p + 1, beside : beside + 1]
        return carry

    middle = (row_of[:, : half + LANE] >= rows // 4) & (row_of[:, : half + LANE] < rows - rows // 4)
    kept = jnp.where(lane_of < SEAM, jnp.where(s == n_sub - 1, 0.0, 1.0), jnp.where(s == 0, 0.0, 1.0)) > 0.5

    def pack(cat, phase):
        cat = jnp.concatenate([jnp.where(kept, cat[:, :LANE], 0.0), cat[:, LANE:]], axis=1)
        cat = pltpu.roll(cat, wide - LANE // 2, 1)
        lower, upper = cat[:, : half + LANE], pltpu.roll(cat[:, half:], rows // 2, 0)
        return jnp.where(middle, lower, upper) if phase == 0 else jnp.where(middle, upper, lower)

    def put(phase, pair, packed):
        both = jnp.concatenate(packed, axis=0).astype(jnp.bfloat16)
        scalars[phase, pl.ds(pl.multiple_of(pair * 2 * rows, 2 * rows), 2 * rows)] = both

    def second_step(pair, carry):
        packed = []
        for p in (2 * pair, 2 * pair + 1):
            new_sub, new_cat = step(mid, p + 1)
            sub_out[p] = new_sub[:, LANE:]
            cat_out[p] = new_cat[:, LANE:]
            wide_cat[p] = new_cat
            packed.append(pack(new_cat, 0))
        put(0, pair, packed)
        return carry

    for copy in z_copies:
        copy.wait_recv()
    lax.fori_loop(1, planes - 1, first_step, 0, unroll=2)
    lax.fori_loop(1, planes // 2 - 1, second_step, 0, unroll=2)

    forwards = []
    for a in range(2):
        here = pl.ds(0 if a == 0 else planes + 2, 2)
        for f in range(2):
            x_copies[2 * a + f].wait_recv()
            for i in range(2):
                p = i if a == 0 else planes + 2 + i
                x_out[a, f, i] = ring_block(raw[f, p, :, first_block], raw[f, p, :, last_block], lane_of)
        copy = remote(x_out.at[a], raw.at[:, here, :, pl.ds(0, LANE)], xf_send.at[a], xf_recv.at[a], partner)
        copy.start()
        forwards.append(copy)
    for copy in forwards:
        copy.wait_recv()
    for a, p in ((0, 1), (1, planes + 2)):
        raw_plane(p)
        first_step(0 if a == 0 else planes - 1, 0)
        for side, (y, _) in enumerate(ends):
            for f in range(2):
                mid_edge[a, side, f : f + 1] = mid[f, p - 1, y : y + 1]
    lax.fori_loop(0, 2, lambda i, carry: second_step(i * (planes // 2 - 1), carry), 0)

    depth_total = float(planes * n_group)
    dim_top = 1.00001 * -math.expm1(-planes * TABLE_TOP / depth_total)
    light_top = TABLE_TOP * dim_top
    g_copies = []

    def render(phase, k):
        def resample(b, carry):
            band = bands[k * sheets + b]
            size = SHEET * rows
            for c in range(half // LANE):
                piece = scalars[phase, pl.ds(pl.multiple_of(b * size, size), size), c * LANE : (c + 2) * LANE]
                out = jnp.dot(piece, band, preferred_element_type=jnp.float32)
                samples[pl.ds(b * SHEET, SHEET), :, 2 * c * LANE : 2 * (c + 1) * LANE] = out.reshape(
                    SHEET, rows, 2 * LANE
                )
            return carry

        lax.fori_loop(0, sheets, resample, 0)

        level_of = lax.broadcasted_iota(jnp.int32, (LEVELS, LANE), 0)
        lines = []
        for which, scale in ((0, -LOG2_E / depth_total), (1, 1.0)):
            values = [table[k, which, l] * scale for l in range(LEVELS)]
            intercepts = jnp.full((LEVELS, LANE), values[LEVELS - 1], jnp.float32)
            slopes = jnp.zeros((LEVELS, LANE), jnp.float32)
            for l in range(LEVELS - 1):
                slope = values[l + 1] - values[l]
                slopes = jnp.where(level_of == l, slope, slopes)
                intercepts = jnp.where(level_of == l, values[l] - l * slope, intercepts)
            lines += [intercepts, slopes]
        ascending = order[k, 1] > order[k, 0]

        def line(which, level, q):
            picked = [
                jnp.take_along_axis(values, level, axis=0, mode="promise_in_bounds")
                for values in lines[2 * which : 2 * which + 2]
            ]
            return picked[0] + picked[1] * q

        starts = range(0, depth, LANE)

        def visit(i, state):
            p = jnp.where(ascending, i, planes - 1 - i)
            after = []
            for start, (light, depth_log, clear) in zip(starts, state):
                q = jnp.clip(samples[p, :, start : start + LANE], 0.0, LEVELS - 1.0)
                level = q.astype(jnp.int32)
                depth_log = depth_log + line(0, level, q)
                left = jnp.exp2(depth_log)
                after.append((light + line(1, level, q) * (clear - left), depth_log, left))
            return tuple(after)

        none = jnp.zeros((rows, LANE), jnp.float32)
        state = lax.fori_loop(
            0, planes, visit, tuple((none, none, none + 1.0) for start in starts), unroll=8
        )
        for start, (light, _, clear) in zip(starts, state):
            slabs[g, phase, k, :, start : start + LANE] = jnp.concatenate(
                [encode(light, light_top), encode(1.0 - clear, dim_top)], axis=0
            )
        for d in range(1, n_group):
            slot = slabs.at[g, phase, k]
            copy = remote(slot, slot, g_send.at[d - 1, phase, k], g_recv.at[d - 1, phase, k], at(dg=d))
            copy.start()
            g_copies.append(copy)

    def finish(phase, k):
        for d in range(1, n_group):
            slot = slabs.at[at(dg=-d)[0], phase, k]
            remote(slot, slot, g_send.at[d - 1, phase, k], g_recv.at[d - 1, phase, k], at(dg=d)).wait_recv()
        total = jnp.zeros((rows, depth), jnp.float32)
        coded = [slabs[slab, phase, k] for slab in range(n_group)]
        lights = [decode(one[:rows], light_top) for one in coded]
        clears = [1.0 - decode(one[rows:], dim_top) for one in coded]
        for slab in range(n_group):
            passed = lights[slab]
            for other in range(n_group):
                if other != slab:
                    ahead = order[k, other] < order[k, slab]
                    passed = passed * jnp.where(ahead, clears[other], 1.0)
            total = total + passed
        return total

    def early(k):
        render(0, k)

    def take_rows():
        for copy in d_copies:
            copy.wait_recv()
        for copy in y_copies[0]:
            copy.wait_recv()
        for a in range(2):
            for b in range(2):
                edge_out[a, b] = ring_block(edge[a, b, :, first_block], edge[a, b, :, last_block], lane_of[:2])
        copies = [
            remote(edge_out, edge.at[:, :, :, pl.ds(0, LANE)], df_send.at[0], df_recv.at[0], partner)
        ]
        for side in range(2):
            for layer in range(3):
                y_out[side, layer] = ring_block(
                    halo_recv[side, layer, :, first_block].astype(jnp.int32),
                    halo_recv[side, layer, :, last_block].astype(jnp.int32), lane_of_planes,
                ).astype(jnp.int16)
            copies.append(
                remote(y_out.at[side], halo_recv.at[side, pl.ds(0, 3), :, pl.ds(0, LANE)],
                       yf_send.at[side], yf_recv.at[side], partner)
            )
        for copy in copies:
            copy.start()
        return copies

    for k in range(views):
        if k == TAKE_AT:
            rows_copies = take_rows()
        early(k)
    if TAKE_AT >= views:
        rows_copies = take_rows()
    for copy in rows_copies:
        copy.wait_recv()
    forwards += rows_copies

    plane_of = lax.broadcasted_iota(jnp.int32, (planes, wide), 0)

    def along_x(x, low, high):
        before = jnp.where(plane_of == 0, jnp.broadcast_to(low, x.shape), pltpu.roll(x, 1, 0))
        after = jnp.where(plane_of == planes - 1, jnp.broadcast_to(high, x.shape), pltpu.roll(x, planes - 1, 0))
        return before + after

    for side in range(2):
        near = [decode(halo_recv[side, f]) for f in range(2)]
        far = (0.0, decode(halo_recv[side, 2]))
        ends_x = [[edge[a, side, f : f + 1] for a in range(2)] for f in range(2)]
        beyond = react(*near, *[
            along_x(near[f], *ends_x[f]) + inner[side, f] + far[f] + along_z(near[f]) for f in range(2)
        ])
        centers, besides = [], []
        for f in range(2):
            center = outer[side, f] + SPREADS[f] * near[f]
            low, high = [mid_edge[a, side, f : f + 1] + SPREADS[f] * ends_x[f][a] for a in range(2)]
            centers.append(center)
            besides.append(along_x(center, low, high) + beyond[f] + second[side, f] + along_z(center))
        new = react(*centers, *besides)
        for f in range(2):
            late[side, 0, f] = new[f]
            late[side, 1, f] = SPREADS[f] * SPREADS[f] * near[f]

    def mended(old, f, p, lanes):
        row = row_of[:, lanes]
        new = [[jnp.broadcast_to(late[side, i, f, pl.ds(p, 1), lanes], old.shape) for i in range(2)] for side in range(2)]
        added = jnp.where(row == 1, new[0][1], jnp.where(row == last - 1, new[1][1], 0.0))
        return jnp.where(row == 0, new[0][0], jnp.where(row == last, new[1][0], old + added))

    def mend_catalyst(pair, carry):
        packed = []
        for p in (2 * pair, 2 * pair + 1):
            new_cat = mended(wide_cat[p], 1, p, slice(0, wide))
            cat_out[p] = new_cat[:, LANE:]
            packed.append(pack(new_cat, 1))
        put(1, pair, packed)
        return carry

    lax.fori_loop(0, planes // 2, mend_catalyst, 0, unroll=2)

    for k in range(views):
        render(1, k)

    for side in range(2):
        y_copies[1][side].wait_recv()
        far = decode(halo_recv[side, 3, :, LANE:wide])
        late[side, 0, 0, :, LANE:wide] = late[side, 0, 0, :, LANE:wide] + SPREADS[0] * SPREADS[0] * far

    def mend_substrate(p, carry):
        sub_out[p] = mended(sub_out[p], 0, p, slice(LANE, wide))
        return carry

    lax.fori_loop(0, planes, mend_substrate, 0, unroll=2)

    middle = middle[:, :1] & (row_of[:, :depth] >= 0)
    for k in range(views):
        mid_rows, end_rows = finish(0, k), finish(1, k)
        images[k, :, :depth] = jnp.where(middle, mid_rows, end_rows)
        images[k, :, depth:] = pltpu.roll(jnp.where(middle, end_rows, mid_rows), rows // 2, 0)

    for copy in started + forwards + g_copies:
        copy.wait_send()


PIECES = 4


def hand_over(*refs):
    sources, targets, (sem,) = refs[:3], refs[3:6], refs[6:]
    copies = [pltpu.make_async_copy(a, b, sem.at[i]) for i, (a, b) in enumerate(zip(sources, targets))]
    for copy in copies:
        copy.start()
    for copy in copies:
        copy.wait()


def solution(mesh):
    counts = (mesh.shape["group"], mesh.shape["tile"], mesh.shape["sub"])

    def local(substrate, catalyst, shear_offsets, slab_order, transfer_table):
        planes, rows, depth = substrate.shape
        views = slab_order.shape[0]
        wide = depth + LANE
        sheets = planes // SHEET
        f32 = jnp.float32
        dma = pltpu.SemaphoreType.DMA
        smem = pl.BlockSpec(memory_space=pltpu.SMEM)
        vmem = pl.BlockSpec(memory_space=pltpu.VMEM)
        hbm = pl.BlockSpec(memory_space=pltpu.HBM)
        anywhere = pl.BlockSpec(memory_space=pl.ANY)
        results = pl.pallas_call(
            functools.partial(kernel, counts),
            out_shape=(
                pltpu.VMEM(substrate.shape, f32),
                pltpu.VMEM(substrate.shape, f32),
                pltpu.VMEM((views, rows, 2 * depth), f32),
            ),
            in_specs=[hbm, hbm, smem, smem, smem],
            out_specs=(vmem, vmem, vmem),
            scratch_shapes=[
                pltpu.VMEM((2, planes + 4, rows, wide), f32),
                pltpu.VMEM((2, planes + 2, rows, wide), f32),
                pltpu.VMEM((2, 4, planes, depth), jnp.int16),
                pltpu.VMEM((2, 4, planes, wide), jnp.int16),
                pltpu.VMEM((2, 4, planes, wide), f32),
                pltpu.VMEM((2, 2, planes, wide), f32),
                pltpu.VMEM((2, 2, planes, wide), f32),
                pltpu.VMEM((2, 2, planes, wide), f32),
                pltpu.VMEM((2, 2, 2, wide), f32),
                pltpu.VMEM((2, 2, 2, planes, wide), f32),
                pltpu.VMEM((planes, rows, wide), f32),
                pltpu.VMEM((2, planes, rows, LANE), f32),
                pltpu.VMEM((2, 2, 2, rows, LANE), f32),
                pltpu.VMEM((2, 3, planes, LANE), jnp.int16),
                pltpu.VMEM((2, 2, 2, depth), f32),
                pltpu.VMEM((2, 2, 2, wide), f32),
                pltpu.VMEM((2, 2, 2, LANE), f32),
                pltpu.VMEM((2, planes * rows, depth // 2 + LANE), jnp.bfloat16),
                pltpu.VMEM((views * sheets, 2 * LANE, 2 * LANE), jnp.bfloat16),
                pltpu.VMEM((planes, rows, depth), f32),
                pltpu.VMEM((counts[0], 2, views, 2 * rows, depth), jnp.int16),
                dma((2,)), dma((2,)), dma((2,)), dma((2, 2)), dma((2, 2)), dma((2,)), dma((2,)),
                dma((2, 2)), dma((2, 2)), dma((2,)), dma((2,)),
                dma((2, 2)), dma((2, 2)), dma((1,)), dma((1,)),
                dma((counts[0] - 1, 2, views)), dma((counts[0] - 1, 2, views)),
            ],
            compiler_params=pltpu.CompilerParams(collective_id=0, has_side_effects=True, vmem_limit_bytes=60 * 2**20),
        )(substrate, catalyst, shear_offsets, slab_order, transfer_table)
        return pl.pallas_call(
            hand_over,
            out_shape=tuple(jax.ShapeDtypeStruct(one.shape, one.dtype) for one in results),
            in_specs=[vmem] * 3,
            out_specs=(anywhere,) * 3,
            scratch_shapes=[dma((3,))],
            compiler_params=pltpu.CompilerParams(vmem_limit_bytes=4 * 2**20),
        )(*results)

    placed = (P("group", "tile", "sub"), P("group", "tile", "sub"), P(), P(), P())
    return jax.shard_map(
        local,
        mesh=mesh,
        in_specs=placed,
        out_specs=(P("group", "tile", "sub"), P("group", "tile", "sub"), P(None, "tile", "sub")),
        check_vma=False,
    )
```

```python
import functools
import math

import jax
import jax.numpy as jnp
from jax import lax
from jax.experimental import pallas as pl
from jax.experimental.pallas import tpu as pltpu
from jax.sharding import PartitionSpec as P

LEVELS = 8
SHEET = 8
LANE = 128
SEAM = 32

SPREAD_FAST = 0.16
SPREAD_SLOW = 0.08
FEED_RATE = 0.04
KILL_RATE = 0.06
TIME_STEP = 1.0

LOG2_E = math.log2(math.e)

CODE_TOP = 65535.0
TABLE_TOP = 3.5
CODE_SHIFT = 32768.0

MESH = pl.DeviceIdType.MESH


def encode(x, bound=1.0):
    return (jnp.round(x * (CODE_TOP / bound)) - CODE_SHIFT).astype(jnp.int32).astype(jnp.int16)


def decode(x, bound=1.0):
    return (x.astype(jnp.int32).astype(jnp.float32) + CODE_SHIFT) * (bound / CODE_TOP)


SPREADS = (TIME_STEP * SPREAD_FAST, TIME_STEP * SPREAD_SLOW)
KEEP_SUB = 1.0 - TIME_STEP * (6.0 * SPREAD_FAST + FEED_RATE)
KEEP_CAT = 1.0 - TIME_STEP * (6.0 * SPREAD_SLOW + FEED_RATE + KILL_RATE)


def react(sub, cat, beside_sub, beside_cat):
    reacting = TIME_STEP * (sub * cat * cat)
    new_sub = (SPREADS[0] * beside_sub + (TIME_STEP * FEED_RATE + KEEP_SUB * sub)) - reacting
    new_cat = (SPREADS[1] * beside_cat + KEEP_CAT * cat) + reacting
    return new_sub, new_cat


def kernel(
    counts,
    sub_in, cat_in, offsets, order, table,
    sub_out, cat_out, images,
    raw, mid, halo_send, halo_recv, halo, inner, outer, second, mid_edge, late, wide_cat,
    z_out, x_out, x_ring, x_in, y_ring, edge_send, edge, scalars, bands, samples, slabs,
    load_sem, z_send, z_recv, x_send, x_recv, y_send, y_recv, d_send, d_recv, g_send, g_recv,
):
    n_group, n_tile, n_sub = counts
    planes, rows, depth = sub_in.shape
    wide = depth + LANE
    own = pl.ds(LANE, depth)
    views = order.shape[0]
    sheets = planes // SHEET
    half = depth // 2
    last = rows - 1
    g, t, s = lax.axis_index("group"), lax.axis_index("tile"), lax.axis_index("sub")

    def at(dg=0, dt=0, ds=0):
        return (
            lax.rem(g + (dg + n_group), n_group),
            lax.rem(t + (dt + n_tile), n_tile),
            lax.rem(s + (ds + n_sub), n_sub),
        )

    partner = at(ds=1)

    barrier = pltpu.get_barrier_semaphore()
    peers = [partner]
    peers += [at(dt=b, ds=c) for b in (-1, 1) for c in (0, 1)]
    peers += [at(dg=a, ds=1) for a in (-1, 1)]
    peers += [at(dg=d) for d in range(1, n_group)]
    for peer in peers:
        pl.semaphore_signal(barrier, inc=1, device_id=peer, device_id_type=MESH)

    inputs = (sub_in, cat_in)
    loads = [
        pltpu.make_async_copy(inputs[f], raw.at[f, pl.ds(2, planes), :, own], load_sem.at[f])
        for f in range(2)
    ]
    for load in loads:
        load.start()

    def ring_block(low, high, lane_of):
        return jnp.where(lane_of < SEAM, low, high)

    lane_of = lax.broadcasted_iota(jnp.int32, (rows, LANE), 1)
    lane_of_planes = lax.broadcasted_iota(jnp.int32, (planes, LANE), 1)
    row_of = lax.broadcasted_iota(jnp.int32, (rows, wide), 0)
    first_block, last_block = slice(LANE, 2 * LANE), slice(depth, depth + LANE)
    ends = ((0, 1), (last, last - 1))

    def band_step(index, carry):
        k = index // sheets
        b = lax.rem(index, sheets)
        shift = offsets[k, g * sheets + b]
        depth_at = lax.broadcasted_iota(jnp.int32, (2 * LANE, 2 * LANE), 0)
        column = lax.broadcasted_iota(jnp.int32, (2 * LANE, 2 * LANE), 1)
        distance = (2 * depth_at - column) + (shift - LANE)
        weight = (LEVELS - 1) * jnp.maximum(0.0, 1.0 - 0.5 * jnp.abs(distance).astype(jnp.float32))
        column_at = pl.multiple_of(k * 2 * LANE, 2 * LANE)
        bands[b, :, pl.ds(column_at, 2 * LANE)] = weight.astype(jnp.bfloat16)
        return carry

    for load in loads:
        load.wait()

    def collect(p, carry):
        for f in range(2):
            z_out[f, p] = ring_block(raw[f, p + 2, :, first_block], raw[f, p + 2, :, last_block], lane_of)
        for side in range(2):
            near, far = ends[1 - side]
            for layer, (f, y) in enumerate(((0, near), (1, near), (1, far), (0, far))):
                halo[side, layer, pl.ds(p, 1), own] = raw[f, p + 2, y : y + 1, LANE:wide]
        return carry

    lax.fori_loop(0, planes, collect, 0, unroll=4)
    for side in range(2):
        for layer in range(4):
            halo_send[side, layer] = encode(halo[side, layer, :, LANE:wide])
            if layer < 3:
                y_ring[side, layer] = encode(ring_block(
                    halo[side, layer, :, first_block], halo[side, layer, :, last_block], lane_of_planes
                ))
    for a in range(2):
        for f in range(2):
            here = slice(planes, planes + 2) if a == 0 else slice(2, 4)
            whole = raw[f, here, :, LANE:wide].reshape(2 * rows, depth)
            x_out[a, f] = encode(whole)
            x_ring[a, f] = encode(z_out[f, here.start - 2 : here.stop - 2].reshape(2 * rows, LANE))

    pl.semaphore_wait(barrier, len(peers))

    def remote(src, dst, send, recv, to):
        return pltpu.make_async_remote_copy(
            src_ref=src, dst_ref=dst, send_sem=send, recv_sem=recv,
            device_id=to, device_id_type=MESH,
        )

    ring = pl.ds(0, LANE)
    y_copies = [
        [
            remote(halo_send.at[side, pl.ds(0, 3)], halo_recv.at[side, pl.ds(0, 3), :, own],
                   y_send.at[0, side], y_recv.at[0, side], at(dt=1 if side == 0 else -1)),
            remote(y_ring.at[side], halo_recv.at[side, pl.ds(0, 3), :, ring],
                   y_send.at[1, side], y_recv.at[1, side], at(dt=1 if side == 0 else -1, ds=1)),
        ]
        for side in range(2)
    ]
    far_copies = [
        remote(halo_send.at[side, 3], halo_recv.at[side, 3, :, own],
               y_send.at[2, side], y_recv.at[2, side], at(dt=1 if side == 0 else -1))
        for side in range(2)
    ]
    x_copies = [
        [
            remote(x_out.at[a], x_in.at[a, :, :, own], x_send.at[0, a], x_recv.at[0, a], at(dg=1 if a == 0 else -1)),
            remote(x_ring.at[a], x_in.at[a, :, :, ring], x_send.at[1, a], x_recv.at[1, a],
                   at(dg=1 if a == 0 else -1, ds=1)),
        ]
        for a in range(2)
    ]
    z_copies = [
        remote(z_out.at[f], raw.at[f, pl.ds(2, planes), :, ring], z_send.at[f], z_recv.at[f], partner)
        for f in range(2)
    ]
    corner_copies = [
        remote(edge_send.at[side], edge.at[side], d_send.at[side], d_recv.at[side], at(dt=1 if side == 0 else -1))
        for side in range(2)
    ]
    started = z_copies + y_copies[0] + y_copies[1] + x_copies[0] + x_copies[1] + far_copies
    for copy in started:
        copy.start()

    lax.fori_loop(0, views * sheets, band_step, 0)

    def along_z(x):
        return pltpu.roll(x, 1, 1) + pltpu.roll(x, wide - 1, 1)

    def along_y(x):
        below = jnp.where(row_of == 0, 0.0, pltpu.roll(x, 1, 0))
        above = jnp.where(row_of == last, 0.0, pltpu.roll(x, last, 0))
        return below + above

    def step(field, p):
        centers = [field[f, p] for f in range(2)]
        besides = [
            field[f, p + 1] + field[f, p - 1] + along_y(centers[f]) + along_z(centers[f]) for f in range(2)
        ]
        return react(centers[0], centers[1], besides[0], besides[1])

    def raw_plane(p):
        new = step(raw, p)
        for f in range(2):
            mid[f, p - 1] = new[f]

    def first_step(p, carry):
        raw_plane(p + 2)
        for side, (y, beside) in enumerate(ends):
            for f in range(2):
                inner[side, f, pl.ds(p, 1)] = raw[f, p + 2, y : y + 1]
                outer[side, f, pl.ds(p, 1)] = mid[f, p + 1, y : y + 1]
                second[side, f, pl.ds(p, 1)] = mid[f, p + 1, beside : beside + 1]
        return carry

    middle = (row_of[:, : half + LANE] >= rows // 4) & (row_of[:, : half + LANE] < rows - rows // 4)
    kept = jnp.where(lane_of < SEAM, jnp.where(s == n_sub - 1, 0.0, 1.0), jnp.where(s == 0, 0.0, 1.0)) > 0.5

    def pack(cat, phase):
        cat = jnp.concatenate([jnp.where(kept, cat[:, :LANE], 0.0), cat[:, LANE:]], axis=1)
        cat = pltpu.roll(cat, wide - LANE // 2, 1)
        lower, upper = cat[:, : half + LANE], pltpu.roll(cat[:, half:], rows // 2, 0)
        return jnp.where(middle, lower, upper) if phase == 0 else jnp.where(middle, upper, lower)

    def put(phase, pair, packed):
        both = jnp.concatenate(packed, axis=0).astype(jnp.bfloat16)
        start = pair * 2 * rows if phase else pl.multiple_of(pair * 2 * rows, 2 * rows)
        scalars[phase, pl.ds(start, 2 * rows)] = both

    def second_step(pair, carry):
        packed = []
        for p in (2 * pair, 2 * pair + 1):
            new_sub, new_cat = step(mid, p + 1)
            sub_out[p] = new_sub[:, LANE:]
            cat_out[p] = new_cat[:, LANE:]
            wide_cat[p] = new_cat
            packed.append(pack(new_cat, 0))
        put(0, pair, packed)
        return carry

    for copy in z_copies:
        copy.wait_recv()
    lax.fori_loop(1, planes - 1, first_step, 0, unroll=2)
    lax.fori_loop(1, planes // 2 - 1, second_step, 0, unroll=2)

    def resample(phase, blocks):
        size = SHEET * rows
        pieces = half // LANE
        for b in blocks:
            spots = slice(b * size, (b + 1) * size)
            piece = jnp.concatenate(
                [scalars[phase, spots, c * LANE : (c + 2) * LANE] for c in range(pieces)], axis=0
            )
            out = jnp.dot(piece, bands[b], preferred_element_type=jnp.float32)
            for k in range(views):
                for c in range(pieces):
                    samples[k, b * SHEET : (b + 1) * SHEET, :, 2 * c * LANE : 2 * (c + 1) * LANE] = out[
                        c * size : (c + 1) * size, 2 * k * LANE : 2 * (k + 1) * LANE
                    ].reshape(SHEET, rows, 2 * LANE)

    resample(0, range(1, sheets - 1))

    for a in range(2):
        for copy in x_copies[a]:
            copy.wait_recv()
        for f in range(2):
            come = decode(x_in[a, f]).reshape(2, rows, wide)
            start = 0 if a == 0 else planes + 2
            raw[f, start : start + 2] = come
            for side in range(2):
                y, _ = ends[1 - side]
                edge_send[side, a, f : f + 1] = come[1 - a, y : y + 1]
    for copy in corner_copies:
        copy.start()
    for a, p in ((0, 1), (1, planes + 2)):
        raw_plane(p)
        first_step(0 if a == 0 else planes - 1, 0)
        for side, (y, _) in enumerate(ends):
            for f in range(2):
                mid_edge[a, side, f : f + 1] = mid[f, p - 1, y : y + 1]
    lax.fori_loop(0, 2, lambda i, carry: second_step(i * (planes // 2 - 1), carry), 0)

    depth_total = float(planes * n_group)
    dim_top = 1.00001 * -math.expm1(-planes * TABLE_TOP / depth_total)
    light_top = TABLE_TOP * dim_top
    g_copies = []

    def render(phase, k):
        level_of = lax.broadcasted_iota(jnp.int32, (LEVELS, LANE), 0)
        lines = []
        for which, scale in ((0, -LOG2_E / depth_total), (1, 1.0)):
            values = [table[k, which, l] * scale for l in range(LEVELS)]
            intercepts = jnp.full((LEVELS, LANE), values[LEVELS - 1], jnp.float32)
            slopes = jnp.zeros((LEVELS, LANE), jnp.float32)
            for l in range(LEVELS - 1):
                slope = values[l + 1] - values[l]
                slopes = jnp.where(level_of == l, slope, slopes)
                intercepts = jnp.where(level_of == l, values[l] - l * slope, intercepts)
            lines += [intercepts, slopes]
        ascending = order[k, 1] > order[k, 0]

        def line(which, level, q):
            picked = [
                jnp.take_along_axis(values, level, axis=0, mode="promise_in_bounds")
                for values in lines[2 * which : 2 * which + 2]
            ]
            return picked[0] + picked[1] * q

        starts = range(0, depth, LANE)

        def visit(i, state):
            p = jnp.where(ascending, i, planes - 1 - i)
            after = []
            for start, (light, depth_log, clear) in zip(starts, state):
                q = jnp.clip(samples[k, p, :, start : start + LANE], 0.0, LEVELS - 1.0)
                level = q.astype(jnp.int32)
                depth_log = depth_log + line(0, level, q)
                left = jnp.exp2(depth_log)
                after.append((light + line(1, level, q) * (clear - left), depth_log, left))
            return tuple(after)

        none = jnp.zeros((rows, LANE), jnp.float32)
        state = lax.fori_loop(
            0, planes, visit, tuple((none, none, none + 1.0) for start in starts), unroll=8
        )
        for start, (light, _, clear) in zip(starts, state):
            slabs[g, phase, k, :, start : start + LANE] = jnp.concatenate(
                [encode(light, light_top), encode(1.0 - clear, dim_top)], axis=0
            )
        for d in range(1, n_group):
            slot = slabs.at[g, phase, k]
            copy = remote(slot, slot, g_send.at[d - 1, phase, k], g_recv.at[d - 1, phase, k], at(dg=d))
            copy.start()
            g_copies.append(copy)

    def finish(phase, k):
        for d in range(1, n_group):
            slot = slabs.at[at(dg=-d)[0], phase, k]
            remote(slot, slot, g_send.at[d - 1, phase, k], g_recv.at[d - 1, phase, k], at(dg=d)).wait_recv()
        total = jnp.zeros((rows, depth), jnp.float32)
        coded = [slabs[slab, phase, k] for slab in range(n_group)]
        lights = [decode(one[:rows], light_top) for one in coded]
        clears = [1.0 - decode(one[rows:], dim_top) for one in coded]
        for slab in range(n_group):
            passed = lights[slab]
            for other in range(n_group):
                if other != slab:
                    ahead = order[k, other] < order[k, slab]
                    passed = passed * jnp.where(ahead, clears[other], 1.0)
            total = total + passed
        return total

    resample(0, (0, sheets - 1))
    for k in range(views):
        render(0, k)

    for side in range(2):
        for copy in y_copies[side]:
            copy.wait_recv()

    plane_of = lax.broadcasted_iota(jnp.int32, (planes, wide), 0)

    def along_x(x, low=None, high=None):
        low = 0.0 if low is None else jnp.broadcast_to(low, x.shape)
        high = 0.0 if high is None else jnp.broadcast_to(high, x.shape)
        before = jnp.where(plane_of == 0, low, pltpu.roll(x, 1, 0))
        after = jnp.where(plane_of == planes - 1, high, pltpu.roll(x, planes - 1, 0))
        return before + after

    def outer_row(side, f, far):
        near = [decode(halo_recv[side, h]) for h in range(2)]
        center = [outer[side, h] + SPREADS[h] * near[h] for h in range(2)]
        beyond = react(*near, *[along_x(near[f]) + inner[side, f] + along_z(near[f])] * 2)[f]
        beyond = beyond + SPREADS[f] * far
        beside = along_x(center[f], *[mid_edge[a, side, f : f + 1] for a in range(2)])
        beside = beside + beyond + second[side, f] + along_z(center[f])
        late[side, 0, f] = react(*center, beside, beside)[f]
        late[side, 1, f] = SPREADS[f] * SPREADS[f] * near[f]

    def add_corners(f):
        for side in range(2):
            for a, p in ((0, 0), (1, planes - 1)):
                late[side, 0, f, p : p + 1] = (
                    late[side, 0, f, p : p + 1] + 2.0 * SPREADS[f] * SPREADS[f] * edge[side, a, f : f + 1]
                )

    for side in range(2):
        outer_row(side, 1, decode(halo_recv[side, 2]))

    def mended(old, f, p, lanes):
        row = row_of[:, lanes]
        new = [[jnp.broadcast_to(late[side, i, f, pl.ds(p, 1), lanes], old.shape) for i in range(2)] for side in range(2)]
        added = jnp.where(row == 1, new[0][1], jnp.where(row == last - 1, new[1][1], 0.0))
        return jnp.where(row == 0, new[0][0], jnp.where(row == last, new[1][0], old + added))

    def mend_catalyst(pair):
        packed = []
        for p in (2 * pair, 2 * pair + 1):
            new_cat = mended(wide_cat[p], 1, p, slice(0, wide))
            cat_out[p] = new_cat[:, LANE:]
            packed.append(pack(new_cat, 1))
        put(1, pair, packed)

    for b in (*range(1, sheets - 1), 0, sheets - 1):
        if b == 0:
            for copy in corner_copies:
                copy.wait_recv()
            add_corners(1)
        for pair in range(SHEET // 2):
            mend_catalyst(b * (SHEET // 2) + pair)
        resample(1, (b,))

    for k in range(views):
        render(1, k)

    for side in range(2):
        far_copies[side].wait_recv()
        far = decode(halo_recv[side, 3, :, LANE:wide])
        outer_row(side, 0, jnp.concatenate([jnp.zeros((planes, LANE), jnp.float32), far], axis=1))
    add_corners(0)

    def mend_substrate(p, carry):
        sub_out[p] = mended(sub_out[p], 0, p, slice(LANE, wide))
        return carry

    lax.fori_loop(0, planes, mend_substrate, 0, unroll=2)

    middle = middle[:, :1] & (row_of[:, :depth] >= 0)
    for k in range(views):
        mid_rows, end_rows = finish(0, k), finish(1, k)
        images[k, :, :depth] = jnp.where(middle, mid_rows, end_rows)
        images[k, :, depth:] = pltpu.roll(jnp.where(middle, end_rows, mid_rows), rows // 2, 0)

    for copy in started + corner_copies + g_copies:
        copy.wait_send()


PIECES = 4


def hand_over(*refs):
    sources, targets, (sem,) = refs[:3], refs[3:6], refs[6:]
    copies = [pltpu.make_async_copy(a, b, sem.at[i]) for i, (a, b) in enumerate(zip(sources, targets))]
    for copy in copies:
        copy.start()
    for copy in copies:
        copy.wait()


def solution(mesh):
    counts = (mesh.shape["group"], mesh.shape["tile"], mesh.shape["sub"])

    def local(substrate, catalyst, shear_offsets, slab_order, transfer_table):
        planes, rows, depth = substrate.shape
        views = slab_order.shape[0]
        wide = depth + LANE
        sheets = planes // SHEET
        f32 = jnp.float32
        dma = pltpu.SemaphoreType.DMA
        smem = pl.BlockSpec(memory_space=pltpu.SMEM)
        vmem = pl.BlockSpec(memory_space=pltpu.VMEM)
        hbm = pl.BlockSpec(memory_space=pltpu.HBM)
        anywhere = pl.BlockSpec(memory_space=pl.ANY)
        results = pl.pallas_call(
            functools.partial(kernel, counts),
            out_shape=(
                pltpu.VMEM(substrate.shape, f32),
                pltpu.VMEM(substrate.shape, f32),
                pltpu.VMEM((views, rows, 2 * depth), f32),
            ),
            in_specs=[hbm, hbm, smem, smem, smem],
            out_specs=(vmem, vmem, vmem),
            scratch_shapes=[
                pltpu.VMEM((2, planes + 4, rows, wide), f32),
                pltpu.VMEM((2, planes + 2, rows, wide), f32),
                pltpu.VMEM((2, 4, planes, depth), jnp.int16),
                pltpu.VMEM((2, 4, planes, wide), jnp.int16),
                pltpu.VMEM((2, 4, planes, wide), f32),
                pltpu.VMEM((2, 2, planes, wide), f32),
                pltpu.VMEM((2, 2, planes, wide), f32),
                pltpu.VMEM((2, 2, planes, wide), f32),
                pltpu.VMEM((2, 2, 2, wide), f32),
                pltpu.VMEM((2, 2, 2, planes, wide), f32),
                pltpu.VMEM((planes, rows, wide), f32),
                pltpu.VMEM((2, planes, rows, LANE), f32),
                pltpu.VMEM((2, 2, 2 * rows, depth), jnp.int16),
                pltpu.VMEM((2, 2, 2 * rows, LANE), jnp.int16),
                pltpu.VMEM((2, 2, 2 * rows, wide), jnp.int16),
                pltpu.VMEM((2, 3, planes, LANE), jnp.int16),
                pltpu.VMEM((2, 2, 2, wide), f32),
                pltpu.VMEM((2, 2, 2, wide), f32),
                pltpu.VMEM((2, planes * rows, depth // 2 + LANE), jnp.bfloat16),
                pltpu.VMEM((sheets, 2 * LANE, views * 2 * LANE), jnp.bfloat16),
                pltpu.VMEM((views, planes, rows, depth), f32),
                pltpu.VMEM((counts[0], 2, views, 2 * rows, depth), jnp.int16),
                dma((2,)), dma((2,)), dma((2,)), dma((2, 2)), dma((2, 2)), dma((3, 2)), dma((3, 2)),
                dma((2,)), dma((2,)),
                dma((counts[0] - 1, 2, views)), dma((counts[0] - 1, 2, views)),
            ],
            compiler_params=pltpu.CompilerParams(collective_id=0, has_side_effects=True, vmem_limit_bytes=60 * 2**20),
        )(substrate, catalyst, shear_offsets, slab_order, transfer_table)
        return pl.pallas_call(
            hand_over,
            out_shape=tuple(jax.ShapeDtypeStruct(one.shape, one.dtype) for one in results),
            in_specs=[vmem] * 3,
            out_specs=(anywhere,) * 3,
            scratch_shapes=[dma((3,))],
            compiler_params=pltpu.CompilerParams(vmem_limit_bytes=4 * 2**20),
        )(*results)

    placed = (P("group", "tile", "sub"), P("group", "tile", "sub"), P(), P(), P())
    return jax.shard_map(
        local,
        mesh=mesh,
        in_specs=placed,
        out_specs=(P("group", "tile", "sub"), P("group", "tile", "sub"), P(None, "tile", "sub")),
        check_vma=False,
    )
```

```python
import functools
import math

import jax
import jax.numpy as jnp
from jax import lax
from jax.experimental import pallas as pl
from jax.experimental.pallas import tpu as pltpu
from jax.sharding import PartitionSpec as P

LEVELS = 8
SHEET = 8
LANE = 128
SEAM = 32
PACK = 16
LOADS = 2

SPREAD_FAST = 0.16
SPREAD_SLOW = 0.08
FEED_RATE = 0.04
KILL_RATE = 0.06
TIME_STEP = 1.0

LOG2_E = math.log2(math.e)

CODE_TOP = 65535.0
TABLE_TOP = 3.5
CODE_SHIFT = 32768.0

MESH = pl.DeviceIdType.MESH


def encode(x, bound=1.0):
    return (jnp.round(x * (CODE_TOP / bound)) - CODE_SHIFT).astype(jnp.int32).astype(jnp.int16)


def decode(x, bound=1.0):
    return (x.astype(jnp.int32).astype(jnp.float32) + CODE_SHIFT) * (bound / CODE_TOP)


SPREADS = (TIME_STEP * SPREAD_FAST, TIME_STEP * SPREAD_SLOW)
KEEP_SUB = 1.0 - TIME_STEP * (6.0 * SPREAD_FAST + FEED_RATE)
KEEP_CAT = 1.0 - TIME_STEP * (6.0 * SPREAD_SLOW + FEED_RATE + KILL_RATE)


def react(sub, cat, beside_sub, beside_cat):
    reacting = TIME_STEP * (sub * cat * cat)
    new_sub = (SPREADS[0] * beside_sub + (TIME_STEP * FEED_RATE + KEEP_SUB * sub)) - reacting
    new_cat = (SPREADS[1] * beside_cat + KEEP_CAT * cat) + reacting
    return new_sub, new_cat


def kernel(
    counts,
    sub_in, cat_in, offsets, order, table,
    sub_out, cat_out, images,
    raw, mid, halo_send, halo_recv, halo, inner, outer, second, mid_edge, late, wide_cat,
    z_out, x_out, x_ring, x_in, y_ring, rim_out, rim_ring, rim, edge, scalars, bands, samples, inside, slabs,
    load_sem, z_send, z_recv, x_send, x_recv, y_send, y_recv, c_send, c_recv, d_send, d_recv, g_send, g_recv,
):
    n_group, n_tile, n_sub = counts
    planes, rows, depth = sub_in.shape
    wide = depth + LANE
    own = pl.ds(LANE, depth)
    views = order.shape[0]
    sheets = planes // SHEET
    half = depth // 2
    last = rows - 1
    g, t, s = lax.axis_index("group"), lax.axis_index("tile"), lax.axis_index("sub")

    def at(dg=0, dt=0, ds=0):
        return (
            lax.rem(g + (dg + n_group), n_group),
            lax.rem(t + (dt + n_tile), n_tile),
            lax.rem(s + (ds + n_sub), n_sub),
        )

    partner = at(ds=1)

    barrier = pltpu.get_barrier_semaphore()
    peers = [partner]
    peers += [at(dt=b, ds=c) for b in (-1, 1) for c in (0, 1)]
    peers += [at(dg=a, ds=1) for a in (-1, 1)]
    peers += [at(dg=d) for d in range(1, n_group)]
    for peer in peers:
        pl.semaphore_signal(barrier, inc=1, device_id=peer, device_id_type=MESH)

    inputs = (sub_in, cat_in)
    pieces = math.gcd(planes // PACK, LOADS)
    piece = planes // pieces
    loads = [
        [
            pltpu.make_async_copy(
                inputs[f].at[pl.ds(i * piece, piece)], raw.at[f, pl.ds(2 + i * piece, piece), :, own], load_sem.at[i, f]
            )
            for f in range(2)
        ]
        for i in range(pieces)
    ]
    for load in sum(loads, []):
        load.start()

    def ring_block(low, high, lane_of):
        return jnp.where(lane_of < SEAM, low, high)

    lane_of = lax.broadcasted_iota(jnp.int32, (rows, LANE), 1)
    lane_of_planes = lax.broadcasted_iota(jnp.int32, (planes, LANE), 1)
    row_of = lax.broadcasted_iota(jnp.int32, (rows, wide), 0)
    first_block, last_block = slice(LANE, 2 * LANE), slice(depth, depth + LANE)
    ends = ((0, 1), (last, last - 1))

    def band_step(index, carry):
        k = index // sheets
        b = lax.rem(index, sheets)
        shift = offsets[k, g * sheets + b]
        depth_at = lax.broadcasted_iota(jnp.int32, (2 * LANE, 2 * LANE), 0)
        column = lax.broadcasted_iota(jnp.int32, (2 * LANE, 2 * LANE), 1)
        distance = (2 * depth_at - column) + (shift - LANE)
        weight = (LEVELS - 1) * jnp.maximum(0.0, 1.0 - 0.5 * jnp.abs(distance).astype(jnp.float32))
        column_at = pl.multiple_of(k * 2 * LANE, 2 * LANE)
        bands[b, :, pl.ds(column_at, 2 * LANE)] = weight.astype(jnp.bfloat16)
        return carry

    def collect(p, carry):
        for side in range(2):
            near, far = ends[1 - side]
            for layer, (f, y) in enumerate(((0, near), (1, near), (1, far), (0, far))):
                halo[side, layer, pl.ds(p, 1), own] = raw[f, p + 2, y : y + 1, LANE:wide]
        return carry

    for i in range(pieces):
        for load in loads[i]:
            load.wait()
        lax.fori_loop(i * piece, (i + 1) * piece, collect, 0, unroll=4)
        here = slice(i * piece, (i + 1) * piece)
        for side in range(2):
            for layer in range(4):
                halo_send[side, layer, here] = encode(halo[side, layer, here, LANE:wide])
                if layer < 3:
                    y_ring[side, layer, here] = encode(ring_block(
                        halo[side, layer, here, first_block], halo[side, layer, here, last_block],
                        lane_of_planes[here],
                    ))

    def ring_of(f, p):
        return ring_block(raw[f, p + 2, :, first_block], raw[f, p + 2, :, last_block], lane_of)

    for a, p in ((0, planes - 1), (1, 0)):
        for f in range(2):
            around = ring_of(f, p)
            for b in range(2):
                y, _ = ends[1 - b]
                rim_out[a, b, f : f + 1] = raw[f, p + 2, y : y + 1, LANE:wide]
                rim_ring[a, b, f : f + 1] = around[y : y + 1]

    pl.semaphore_wait(barrier, len(peers))

    def remote(src, dst, send, recv, to):
        return pltpu.make_async_remote_copy(
            src_ref=src, dst_ref=dst, send_sem=send, recv_sem=recv,
            device_id=to, device_id_type=MESH,
        )

    ring = pl.ds(0, LANE)
    y_copies = [
        [
            remote(halo_send.at[side, pl.ds(0, 3)], halo_recv.at[side, pl.ds(0, 3), :, own],
                   y_send.at[0, side], y_recv.at[0, side], at(dt=1 if side == 0 else -1)),
            remote(y_ring.at[side], halo_recv.at[side, pl.ds(0, 3), :, ring],
                   y_send.at[1, side], y_recv.at[1, side], at(dt=1 if side == 0 else -1, ds=1)),
        ]
        for side in range(2)
    ]
    far_copies = [
        remote(halo_send.at[side, 3], halo_recv.at[side, 3, :, own],
               y_send.at[2, side], y_recv.at[2, side], at(dt=1 if side == 0 else -1))
        for side in range(2)
    ]
    x_copies = [
        [
            remote(x_out.at[a], x_in.at[a, :, :, own], x_send.at[0, a], x_recv.at[0, a], at(dg=1 if a == 0 else -1)),
            remote(x_ring.at[a], x_in.at[a, :, :, ring], x_send.at[1, a], x_recv.at[1, a],
                   at(dg=1 if a == 0 else -1, ds=1)),
        ]
        for a in range(2)
    ]
    z_copies = [
        remote(z_out.at[f], raw.at[f, pl.ds(2, planes), :, ring], z_send.at[f], z_recv.at[f], partner)
        for f in range(2)
    ]
    rim_copies = [
        copy
        for a in range(2)
        for copy in (
            remote(rim_out.at[a], rim.at[a, :, :, own], c_send.at[0, a], c_recv.at[0, a], at(dg=1 if a == 0 else -1)),
            remote(rim_ring.at[a], rim.at[a, :, :, ring], c_send.at[1, a], c_recv.at[1, a],
                   at(dg=1 if a == 0 else -1, ds=1)),
        )
    ]
    corner_copies = [
        remote(rim.at[a, b], edge.at[b, a], d_send.at[a, b], d_recv.at[a, b], at(dt=1 if b == 0 else -1))
        for a in range(2) for b in range(2)
    ]

    for copy in rim_copies:
        copy.start()
    for copy in y_copies[0] + y_copies[1]:
        copy.start()
    def ring_step(p, carry):
        for f in range(2):
            z_out[f, p] = ring_of(f, p)
        return carry

    lax.fori_loop(0, planes, ring_step, 0, unroll=4)
    for copy in z_copies:
        copy.start()
    for a in range(2):
        for f in range(2):
            here = slice(planes, planes + 2) if a == 0 else slice(2, 4)
            whole = raw[f, here, :, LANE:wide].reshape(2 * rows, depth)
            x_out[a, f] = encode(whole)
            x_ring[a, f] = encode(z_out[f, here.start - 2 : here.stop - 2].reshape(2 * rows, LANE))
    for copy in x_copies[0] + x_copies[1]:
        copy.start()


    def along_z(x):
        return pltpu.roll(x, 1, 1) + pltpu.roll(x, wide - 1, 1)

    def along_y(x):
        below = jnp.where(row_of == 0, 0.0, pltpu.roll(x, 1, 0))
        above = jnp.where(row_of == last, 0.0, pltpu.roll(x, last, 0))
        return below + above

    def step(field, p):
        centers = [field[f, p] for f in range(2)]
        besides = [
            field[f, p + 1] + field[f, p - 1] + along_y(centers[f]) + along_z(centers[f]) for f in range(2)
        ]
        return react(centers[0], centers[1], besides[0], besides[1])

    def raw_plane(p):
        new = step(raw, p)
        for f in range(2):
            mid[f, p - 1] = new[f]

    def first_step(p, carry):
        raw_plane(p + 2)
        for side, (y, beside) in enumerate(ends):
            for f in range(2):
                inner[side, f, pl.ds(p, 1)] = raw[f, p + 2, y : y + 1]
                outer[side, f, pl.ds(p, 1)] = mid[f, p + 1, y : y + 1]
                second[side, f, pl.ds(p, 1)] = mid[f, p + 1, beside : beside + 1]
        return carry

    middle = (row_of[:, : half + LANE] >= rows // 4) & (row_of[:, : half + LANE] < rows - rows // 4)
    kept = jnp.where(lane_of < SEAM, jnp.where(s == n_sub - 1, 0.0, 1.0), jnp.where(s == 0, 0.0, 1.0)) > 0.5

    def pack(cat, phase):
        cat = jnp.concatenate([jnp.where(kept, cat[:, :LANE], 0.0), cat[:, LANE:]], axis=1)
        cat = pltpu.roll(cat, wide - LANE // 2, 1)
        lower, upper = cat[:, : half + LANE], pltpu.roll(cat[:, half:], rows // 2, 0)
        return jnp.where(middle, lower, upper) if phase == 0 else jnp.where(middle, upper, lower)

    def put(phase, pair, packed):
        both = jnp.concatenate(packed, axis=0).astype(jnp.bfloat16)
        start = pair * 2 * rows if phase else pl.multiple_of(pair * 2 * rows, 2 * rows)
        scalars[phase, pl.ds(start, 2 * rows)] = both

    def second_step(pair, carry):
        packed = []
        for p in (2 * pair, 2 * pair + 1):
            new_sub, new_cat = step(mid, p + 1)
            sub_out[p] = new_sub[:, LANE:]
            cat_out[p] = new_cat[:, LANE:]
            wide_cat[p] = new_cat
            packed.append(pack(new_cat, 0))
        put(0, pair, packed)
        return carry

    for copy in z_copies:
        copy.wait_recv()
    lax.fori_loop(1, planes - 1, first_step, 0, unroll=2)
    for copy in rim_copies:
        copy.wait_recv()
    for copy in corner_copies + far_copies:
        copy.start()
    lax.fori_loop(planes - 1, planes - 1, first_step, 0, unroll=2)
    lax.fori_loop(0, views * sheets, band_step, 0)
    lax.fori_loop(1, planes // 2 - 1, second_step, 0, unroll=2)

    def resample(phase, blocks):
        size = SHEET * rows
        pieces = half // LANE
        for b in blocks:
            spots = slice(b * size, (b + 1) * size)
            piece = jnp.concatenate(
                [scalars[phase, spots, c * LANE : (c + 2) * LANE] for c in range(pieces)], axis=0
            )
            out = jnp.dot(piece, bands[b], preferred_element_type=jnp.float32)
            for k in range(views):
                for c in range(pieces):
                    samples[k, b * SHEET : (b + 1) * SHEET, :, 2 * c * LANE : 2 * (c + 1) * LANE] = out[
                        c * size : (c + 1) * size, 2 * k * LANE : 2 * (k + 1) * LANE
                    ].reshape(SHEET, rows, 2 * LANE)

    resample(0, range(1, sheets - 1))
    depth_total = float(planes * n_group)
    dim_top = 1.00001 * -math.expm1(-planes * TABLE_TOP / depth_total)
    light_top = TABLE_TOP * dim_top
    g_copies = []

    def visitor(k):
        level_of = lax.broadcasted_iota(jnp.int32, (LEVELS, LANE), 0)
        lines = []
        for which, scale in ((0, -LOG2_E / depth_total), (1, 1.0)):
            values = [table[k, which, l] * scale for l in range(LEVELS)]
            intercepts = jnp.full((LEVELS, LANE), values[LEVELS - 1], jnp.float32)
            slopes = jnp.zeros((LEVELS, LANE), jnp.float32)
            for l in range(LEVELS - 1):
                slope = values[l + 1] - values[l]
                slopes = jnp.where(level_of == l, slope, slopes)
                intercepts = jnp.where(level_of == l, values[l] - l * slope, intercepts)
            lines += [intercepts, slopes]
        ascending = order[k, 1] > order[k, 0]

        def line(which, level, q):
            picked = [
                jnp.take_along_axis(values, level, axis=0, mode="promise_in_bounds")
                for values in lines[2 * which : 2 * which + 2]
            ]
            return picked[0] + picked[1] * q

        def visit(i, state):
            p = jnp.where(ascending, i, planes - 1 - i)
            after = []
            for start, (light, depth_log, clear) in zip(starts, state):
                q = jnp.clip(samples[k, p, :, start : start + LANE], 0.0, LEVELS - 1.0)
                level = q.astype(jnp.int32)
                depth_log = depth_log + line(0, level, q)
                left = jnp.exp2(depth_log)
                after.append((light + line(1, level, q) * (clear - left), depth_log, left))
            return tuple(after)

        return visit

    starts = range(0, depth, LANE)
    none = jnp.zeros((rows, LANE), jnp.float32)
    fresh = tuple((none, none, none + 1.0) for start in starts)

    def render_inside(k):
        state = lax.fori_loop(SHEET, planes - SHEET, visitor(k), fresh, unroll=8)
        for start, (light, depth_log, _) in zip(starts, state):
            inside[k, 0, :, start : start + LANE] = light
            inside[k, 1, :, start : start + LANE] = depth_log

    def render(phase, k):
        visit = visitor(k)
        state = lax.fori_loop(0, SHEET, visit, fresh, unroll=8)
        after = []
        for start, (light, depth_log, clear) in zip(starts, state):
            light = light + clear * inside[k, 0, :, start : start + LANE]
            depth_log = depth_log + inside[k, 1, :, start : start + LANE]
            after.append((light, depth_log, jnp.exp2(depth_log)))
        state = lax.fori_loop(planes - SHEET, planes, visit, tuple(after), unroll=8)
        for start, (light, _, clear) in zip(starts, state):
            slabs[g, phase, k, :, start : start + LANE] = jnp.concatenate(
                [encode(light, light_top), encode(1.0 - clear, dim_top)], axis=0
            )
        for d in range(1, n_group):
            slot = slabs.at[g, phase, k]
            copy = remote(slot, slot, g_send.at[d - 1, phase, k], g_recv.at[d - 1, phase, k], at(dg=d))
            copy.start()
            g_copies.append(copy)

    for k in range(views):
        render_inside(k)

    for a in range(2):
        for copy in x_copies[a]:
            copy.wait_recv()
        for f in range(2):
            come = decode(x_in[a, f]).reshape(2, rows, wide)
            start = 0 if a == 0 else planes + 2
            raw[f, start : start + 2] = come

    for a, p in ((0, 1), (1, planes + 2)):
        raw_plane(p)
        first_step(0 if a == 0 else planes - 1, 0)
        for side, (y, _) in enumerate(ends):
            for f in range(2):
                mid_edge[a, side, f : f + 1] = mid[f, p - 1, y : y + 1]
    lax.fori_loop(0, 2, lambda i, carry: second_step(i * (planes // 2 - 1), carry), 0)

    def finish(phase, k):
        for d in range(1, n_group):
            slot = slabs.at[at(dg=-d)[0], phase, k]
            remote(slot, slot, g_send.at[d - 1, phase, k], g_recv.at[d - 1, phase, k], at(dg=d)).wait_recv()
        total = jnp.zeros((rows, depth), jnp.float32)
        coded = [slabs[slab, phase, k] for slab in range(n_group)]
        lights = [decode(one[:rows], light_top) for one in coded]
        clears = [1.0 - decode(one[rows:], dim_top) for one in coded]
        for slab in range(n_group):
            passed = lights[slab]
            for other in range(n_group):
                if other != slab:
                    ahead = order[k, other] < order[k, slab]
                    passed = passed * jnp.where(ahead, clears[other], 1.0)
            total = total + passed
        return total

    resample(0, (0, sheets - 1))
    for k in range(views):
        render(0, k)

    for side in range(2):
        for copy in y_copies[side]:
            copy.wait_recv()

    plane_of = lax.broadcasted_iota(jnp.int32, (planes, wide), 0)

    def along_x(x, low=None, high=None):
        low = 0.0 if low is None else jnp.broadcast_to(low, x.shape)
        high = 0.0 if high is None else jnp.broadcast_to(high, x.shape)
        before = jnp.where(plane_of == 0, low, pltpu.roll(x, 1, 0))
        after = jnp.where(plane_of == planes - 1, high, pltpu.roll(x, planes - 1, 0))
        return before + after

    def outer_row(side, f, far):
        near = [decode(halo_recv[side, h]) for h in range(2)]
        center = [outer[side, h] + SPREADS[h] * near[h] for h in range(2)]
        beyond = react(*near, *[along_x(near[f]) + inner[side, f] + along_z(near[f])] * 2)[f]
        beyond = beyond + SPREADS[f] * far
        beside = along_x(center[f], *[mid_edge[a, side, f : f + 1] for a in range(2)])
        beside = beside + beyond + second[side, f] + along_z(center[f])
        late[side, 0, f] = react(*center, beside, beside)[f]
        late[side, 1, f] = SPREADS[f] * SPREADS[f] * near[f]

    def add_corners(f):
        for side in range(2):
            for a, p in ((0, 0), (1, planes - 1)):
                late[side, 0, f, p : p + 1] = (
                    late[side, 0, f, p : p + 1] + 2.0 * SPREADS[f] * SPREADS[f] * edge[side, a, f : f + 1]
                )

    for side in range(2):
        outer_row(side, 1, decode(halo_recv[side, 2]))

    def mended(old, f, p, lanes):
        row = row_of[:, lanes]
        new = [[jnp.broadcast_to(late[side, i, f, pl.ds(p, 1), lanes], old.shape) for i in range(2)] for side in range(2)]
        added = jnp.where(row == 1, new[0][1], jnp.where(row == last - 1, new[1][1], 0.0))
        return jnp.where(row == 0, new[0][0], jnp.where(row == last, new[1][0], old + added))

    def mend_catalyst(pair):
        packed = []
        for p in (2 * pair, 2 * pair + 1):
            new_cat = mended(wide_cat[p], 1, p, slice(0, wide))
            cat_out[p] = new_cat[:, LANE:]
            packed.append(pack(new_cat, 1))
        put(1, pair, packed)

    for b in (*range(1, sheets - 1), 0, sheets - 1):
        if b == 0:
            for k in range(views):
                render_inside(k)
            for copy in corner_copies:
                copy.wait_recv()
            add_corners(1)
        for pair in range(SHEET // 2):
            mend_catalyst(b * (SHEET // 2) + pair)
        resample(1, (b,))

    for k in range(views):
        render(1, k)

    for side in range(2):
        far_copies[side].wait_recv()
        far = decode(halo_recv[side, 3, :, LANE:wide])
        outer_row(side, 0, jnp.concatenate([jnp.zeros((planes, LANE), jnp.float32), far], axis=1))
    add_corners(0)

    def mend_substrate(p, carry):
        sub_out[p] = mended(sub_out[p], 0, p, slice(LANE, wide))
        return carry

    lax.fori_loop(0, planes, mend_substrate, 0, unroll=2)

    middle = middle[:, :1] & (row_of[:, :depth] >= 0)
    for k in range(views):
        mid_rows, end_rows = finish(0, k), finish(1, k)
        images[k, :, :depth] = jnp.where(middle, mid_rows, end_rows)
        images[k, :, depth:] = pltpu.roll(jnp.where(middle, end_rows, mid_rows), rows // 2, 0)

    for copy in y_copies[0] + y_copies[1] + rim_copies + z_copies + x_copies[0] + x_copies[1]:
        copy.wait_send()
    for copy in corner_copies + far_copies + g_copies:
        copy.wait_send()


PIECES = 4


def hand_over(*refs):
    sources, targets, (sem,) = refs[:3], refs[3:6], refs[6:]
    copies = [pltpu.make_async_copy(a, b, sem.at[i]) for i, (a, b) in enumerate(zip(sources, targets))]
    for copy in copies:
        copy.start()
    for copy in copies:
        copy.wait()


def solution(mesh):
    counts = (mesh.shape["group"], mesh.shape["tile"], mesh.shape["sub"])

    def local(substrate, catalyst, shear_offsets, slab_order, transfer_table):
        planes, rows, depth = substrate.shape
        views = slab_order.shape[0]
        wide = depth + LANE
        sheets = planes // SHEET
        f32 = jnp.float32
        dma = pltpu.SemaphoreType.DMA
        smem = pl.BlockSpec(memory_space=pltpu.SMEM)
        vmem = pl.BlockSpec(memory_space=pltpu.VMEM)
        hbm = pl.BlockSpec(memory_space=pltpu.HBM)
        anywhere = pl.BlockSpec(memory_space=pl.ANY)
        results = pl.pallas_call(
            functools.partial(kernel, counts),
            out_shape=(
                pltpu.VMEM(substrate.shape, f32),
                pltpu.VMEM(substrate.shape, f32),
                pltpu.VMEM((views, rows, 2 * depth), f32),
            ),
            in_specs=[hbm, hbm, smem, smem, smem],
            out_specs=(vmem, vmem, vmem),
            scratch_shapes=[
                pltpu.VMEM((2, planes + 4, rows, wide), f32),
                pltpu.VMEM((2, planes + 2, rows, wide), f32),
                pltpu.VMEM((2, 4, planes, depth), jnp.int16),
                pltpu.VMEM((2, 4, planes, wide), jnp.int16),
                pltpu.VMEM((2, 4, planes, wide), f32),
                pltpu.VMEM((2, 2, planes, wide), f32),
                pltpu.VMEM((2, 2, planes, wide), f32),
                pltpu.VMEM((2, 2, planes, wide), f32),
                pltpu.VMEM((2, 2, 2, wide), f32),
                pltpu.VMEM((2, 2, 2, planes, wide), f32),
                pltpu.VMEM((planes, rows, wide), f32),
                pltpu.VMEM((2, planes, rows, LANE), f32),
                pltpu.VMEM((2, 2, 2 * rows, depth), jnp.int16),
                pltpu.VMEM((2, 2, 2 * rows, LANE), jnp.int16),
                pltpu.VMEM((2, 2, 2 * rows, wide), jnp.int16),
                pltpu.VMEM((2, 3, planes, LANE), jnp.int16),
                pltpu.VMEM((2, 2, 2, depth), f32),
                pltpu.VMEM((2, 2, 2, LANE), f32),
                pltpu.VMEM((2, 2, 2, wide), f32),
                pltpu.VMEM((2, 2, 2, wide), f32),
                pltpu.VMEM((2, planes * rows, depth // 2 + LANE), jnp.bfloat16),
                pltpu.VMEM((sheets, 2 * LANE, views * 2 * LANE), jnp.bfloat16),
                pltpu.VMEM((views, planes, rows, depth), f32),
                pltpu.VMEM((views, 2, rows, depth), f32),
                pltpu.VMEM((counts[0], 2, views, 2 * rows, depth), jnp.int16),
                dma((LOADS, 2)), dma((2,)), dma((2,)), dma((2, 2)), dma((2, 2)), dma((3, 2)), dma((3, 2)),
                dma((2, 2)), dma((2, 2)), dma((2, 2)), dma((2, 2)),
                dma((counts[0] - 1, 2, views)), dma((counts[0] - 1, 2, views)),
            ],
            compiler_params=pltpu.CompilerParams(collective_id=0, has_side_effects=True, vmem_limit_bytes=60 * 2**20),
        )(substrate, catalyst, shear_offsets, slab_order, transfer_table)
        return pl.pallas_call(
            hand_over,
            out_shape=tuple(jax.ShapeDtypeStruct(one.shape, one.dtype) for one in results),
            in_specs=[vmem] * 3,
            out_specs=(anywhere,) * 3,
            scratch_shapes=[dma((3,))],
            compiler_params=pltpu.CompilerParams(vmem_limit_bytes=4 * 2**20),
        )(*results)

    placed = (P("group", "tile", "sub"), P("group", "tile", "sub"), P(), P(), P())
    return jax.shard_map(
        local,
        mesh=mesh,
        in_specs=placed,
        out_specs=(P("group", "tile", "sub"), P("group", "tile", "sub"), P(None, "tile", "sub")),
        check_vma=False,
    )
```

```python
import functools
import math

import jax
import jax.numpy as jnp
from jax import lax
from jax.experimental import pallas as pl
from jax.experimental.pallas import tpu as pltpu
from jax.sharding import PartitionSpec as P

LEVELS = 8
SHEET = 8
LANE = 128
SEAM = 32
PACK = 16
LOADS = 2

SPREAD_FAST = 0.16
SPREAD_SLOW = 0.08
FEED_RATE = 0.04
KILL_RATE = 0.06
TIME_STEP = 1.0

LOG2_E = math.log2(math.e)

CODE_TOP = 65535.0
TABLE_TOP = 3.5
CODE_SHIFT = 32768.0

MESH = pl.DeviceIdType.MESH


def encode(x, bound=1.0):
    return (jnp.round(x * (CODE_TOP / bound)) - CODE_SHIFT).astype(jnp.int32).astype(jnp.int16)


def decode(x, bound=1.0):
    return (x.astype(jnp.int32).astype(jnp.float32) + CODE_SHIFT) * (bound / CODE_TOP)


SPREADS = (TIME_STEP * SPREAD_FAST, TIME_STEP * SPREAD_SLOW)
KEEP_SUB = 1.0 - TIME_STEP * (6.0 * SPREAD_FAST + FEED_RATE)
KEEP_CAT = 1.0 - TIME_STEP * (6.0 * SPREAD_SLOW + FEED_RATE + KILL_RATE)


def react(sub, cat, beside_sub, beside_cat):
    reacting = TIME_STEP * (sub * cat * cat)
    new_sub = (SPREADS[0] * beside_sub + (TIME_STEP * FEED_RATE + KEEP_SUB * sub)) - reacting
    new_cat = (SPREADS[1] * beside_cat + KEEP_CAT * cat) + reacting
    return new_sub, new_cat


def kernel(
    counts,
    sub_in, cat_in, offsets, order, table,
    sub_out, cat_out, images,
    raw, mid, halo_send, halo_recv, halo, inner, outer, second, mid_edge, late, wide_cat,
    z_out, x_out, x_ring, x_in, y_ring, rim_out, rim_ring, edge, scalars, bands, samples, inside, slabs,
    load_sem, z_send, z_recv, x_send, x_recv, y_send, y_recv, c_send, c_recv, g_send, g_recv,
):
    n_group, n_tile, n_sub = counts
    planes, rows, depth = sub_in.shape
    wide = depth + LANE
    own = pl.ds(LANE, depth)
    views = order.shape[0]
    sheets = planes // SHEET
    half = depth // 2
    last = rows - 1
    g, t, s = lax.axis_index("group"), lax.axis_index("tile"), lax.axis_index("sub")

    def at(dg=0, dt=0, ds=0):
        return (
            lax.rem(g + (dg + n_group), n_group),
            lax.rem(t + (dt + n_tile), n_tile),
            lax.rem(s + (ds + n_sub), n_sub),
        )

    partner = at(ds=1)

    barrier = pltpu.get_barrier_semaphore()
    peers = [partner]
    peers += [at(dt=b, ds=c) for b in (-1, 1) for c in (0, 1)]
    peers += [at(dg=a, dt=b, ds=c) for a in (-1, 1) for b in (-1, 1) for c in (0, 1)]
    peers += [at(dg=a, ds=1) for a in (-1, 1)]
    peers += [at(dg=d) for d in range(1, n_group)]
    for peer in peers:
        pl.semaphore_signal(barrier, inc=1, device_id=peer, device_id_type=MESH)

    inputs = (sub_in, cat_in)
    pieces = math.gcd(planes // PACK, LOADS)
    piece = planes // pieces
    loads = [
        [
            pltpu.make_async_copy(
                inputs[f].at[pl.ds(i * piece, piece)], raw.at[f, pl.ds(2 + i * piece, piece), :, own], load_sem.at[i, f]
            )
            for f in range(2)
        ]
        for i in range(pieces)
    ]
    for load in sum(loads, []):
        load.start()

    def ring_block(low, high, lane_of):
        return jnp.where(lane_of < SEAM, low, high)

    lane_of = lax.broadcasted_iota(jnp.int32, (rows, LANE), 1)
    lane_of_planes = lax.broadcasted_iota(jnp.int32, (planes, LANE), 1)
    row_of = lax.broadcasted_iota(jnp.int32, (rows, wide), 0)
    first_block, last_block = slice(LANE, 2 * LANE), slice(depth, depth + LANE)
    ends = ((0, 1), (last, last - 1))

    def band_step(index, carry):
        k = index // sheets
        b = lax.rem(index, sheets)
        shift = offsets[k, g * sheets + b]
        depth_at = lax.broadcasted_iota(jnp.int32, (2 * LANE, 2 * LANE), 0)
        column = lax.broadcasted_iota(jnp.int32, (2 * LANE, 2 * LANE), 1)
        distance = (2 * depth_at - column) + (shift - LANE)
        weight = (LEVELS - 1) * jnp.maximum(0.0, 1.0 - 0.5 * jnp.abs(distance).astype(jnp.float32))
        column_at = pl.multiple_of(k * 2 * LANE, 2 * LANE)
        bands[b, :, pl.ds(column_at, 2 * LANE)] = weight.astype(jnp.bfloat16)
        return carry

    lax.fori_loop(0, views * sheets, band_step, 0)

    def collect(p, carry):
        for side in range(2):
            near, far = ends[1 - side]
            for layer, (f, y) in enumerate(((0, near), (1, near), (1, far), (0, far))):
                halo[side, layer, pl.ds(p, 1), own] = raw[f, p + 2, y : y + 1, LANE:wide]
        return carry

    for i in range(pieces):
        for load in loads[i]:
            load.wait()
        lax.fori_loop(i * piece, (i + 1) * piece, collect, 0, unroll=4)
        here = slice(i * piece, (i + 1) * piece)
        for side in range(2):
            for layer in range(4):
                halo_send[side, layer, here] = encode(halo[side, layer, here, LANE:wide])
                if layer < 3:
                    y_ring[side, layer, here] = encode(ring_block(
                        halo[side, layer, here, first_block], halo[side, layer, here, last_block],
                        lane_of_planes[here],
                    ))

    def ring_of(f, p):
        return ring_block(raw[f, p + 2, :, first_block], raw[f, p + 2, :, last_block], lane_of)

    for a, p in ((0, planes - 1), (1, 0)):
        for f in range(2):
            around = ring_of(f, p)
            for b in range(2):
                y, _ = ends[1 - b]
                rim_out[a, b, f : f + 1] = raw[f, p + 2, y : y + 1, LANE:wide]
                rim_ring[a, b, f : f + 1] = around[y : y + 1]

    pl.semaphore_wait(barrier, len(peers))

    def remote(src, dst, send, recv, to):
        return pltpu.make_async_remote_copy(
            src_ref=src, dst_ref=dst, send_sem=send, recv_sem=recv,
            device_id=to, device_id_type=MESH,
        )

    ring = pl.ds(0, LANE)
    y_copies = [
        [
            remote(halo_send.at[side, pl.ds(0, 3)], halo_recv.at[side, pl.ds(0, 3), :, own],
                   y_send.at[0, side], y_recv.at[0, side], at(dt=1 if side == 0 else -1)),
            remote(y_ring.at[side], halo_recv.at[side, pl.ds(0, 3), :, ring],
                   y_send.at[1, side], y_recv.at[1, side], at(dt=1 if side == 0 else -1, ds=1)),
        ]
        for side in range(2)
    ]
    far_copies = [
        remote(halo_send.at[side, 3], halo_recv.at[side, 3, :, own],
               y_send.at[2, side], y_recv.at[2, side], at(dt=1 if side == 0 else -1))
        for side in range(2)
    ]
    x_copies = [
        [
            remote(x_out.at[a], x_in.at[a, :, :, own], x_send.at[0, a], x_recv.at[0, a], at(dg=1 if a == 0 else -1)),
            remote(x_ring.at[a], x_in.at[a, :, :, ring], x_send.at[1, a], x_recv.at[1, a],
                   at(dg=1 if a == 0 else -1, ds=1)),
        ]
        for a in range(2)
    ]
    z_copies = [
        remote(z_out.at[f], raw.at[f, pl.ds(2, planes), :, ring], z_send.at[f], z_recv.at[f], partner)
        for f in range(2)
    ]
    corner_copies = []
    for a in range(2):
        for b in range(2):
            dg, dt = 1 if a == 0 else -1, 1 if b == 0 else -1
            corner_copies += [
                remote(rim_out.at[a, b], edge.at[b, a, :, own], c_send.at[0, a, b], c_recv.at[0, a, b], at(dg=dg, dt=dt)),
                remote(rim_ring.at[a, b], edge.at[b, a, :, ring], c_send.at[1, a, b], c_recv.at[1, a, b],
                       at(dg=dg, dt=dt, ds=1)),
            ]
    for copy in corner_copies:
        copy.start()
    for copy in y_copies[0] + y_copies[1]:
        copy.start()
    def ring_step(p, carry):
        for f in range(2):
            z_out[f, p] = ring_of(f, p)
        return carry

    lax.fori_loop(0, planes, ring_step, 0, unroll=4)
    for copy in z_copies:
        copy.start()
    for a in range(2):
        for f in range(2):
            here = slice(planes, planes + 2) if a == 0 else slice(2, 4)
            whole = raw[f, here, :, LANE:wide].reshape(2 * rows, depth)
            x_out[a, f] = encode(whole)
            x_ring[a, f] = encode(z_out[f, here.start - 2 : here.stop - 2].reshape(2 * rows, LANE))
    for copy in x_copies[0] + x_copies[1]:
        copy.start()
    for copy in far_copies:
        copy.start()


    def along_z(x):
        return pltpu.roll(x, 1, 1) + pltpu.roll(x, wide - 1, 1)

    def along_y(x):
        below = jnp.where(row_of == 0, 0.0, pltpu.roll(x, 1, 0))
        above = jnp.where(row_of == last, 0.0, pltpu.roll(x, last, 0))
        return below + above

    def step(field, p):
        centers = [field[f, p] for f in range(2)]
        besides = [
            field[f, p + 1] + field[f, p - 1] + along_y(centers[f]) + along_z(centers[f]) for f in range(2)
        ]
        return react(centers[0], centers[1], besides[0], besides[1])

    def raw_plane(p):
        new = step(raw, p)
        for f in range(2):
            mid[f, p - 1] = new[f]

    def first_step(p, carry):
        raw_plane(p + 2)
        for side, (y, beside) in enumerate(ends):
            for f in range(2):
                inner[side, f, pl.ds(p, 1)] = raw[f, p + 2, y : y + 1]
                outer[side, f, pl.ds(p, 1)] = mid[f, p + 1, y : y + 1]
            second[side, 1, pl.ds(p, 1)] = mid[1, p + 1, beside : beside + 1]
        return carry

    middle = (row_of[:, : half + LANE] >= rows // 4) & (row_of[:, : half + LANE] < rows - rows // 4)
    kept = jnp.where(lane_of < SEAM, jnp.where(s == n_sub - 1, 0.0, 1.0), jnp.where(s == 0, 0.0, 1.0)) > 0.5

    def pack(cat, phase):
        cat = jnp.concatenate([jnp.where(kept, cat[:, :LANE], 0.0), cat[:, LANE:]], axis=1)
        cat = pltpu.roll(cat, wide - LANE // 2, 1)
        lower, upper = cat[:, : half + LANE], pltpu.roll(cat[:, half:], rows // 2, 0)
        return jnp.where(middle, lower, upper) if phase == 0 else jnp.where(middle, upper, lower)

    def put(phase, pair, packed):
        both = jnp.concatenate(packed, axis=0).astype(jnp.bfloat16)
        start = pair * 2 * rows if phase else pl.multiple_of(pair * 2 * rows, 2 * rows)
        scalars[phase, pl.ds(start, 2 * rows)] = both

    def second_of(f, p):
        centers = [mid[h, p + 1] for h in range(2)]
        beside = mid[f, p + 2] + mid[f, p] + along_y(centers[f]) + along_z(centers[f])
        return react(*centers, beside, beside)[f]

    def second_step(pair, carry):
        packed = []
        for p in (2 * pair, 2 * pair + 1):
            new_cat = second_of(1, p)
            cat_out[p] = new_cat[:, LANE:]
            wide_cat[p] = new_cat
            packed.append(pack(new_cat, 0))
        put(0, pair, packed)
        return carry

    for copy in z_copies:
        copy.wait_recv()
    lax.fori_loop(1, planes - 1, first_step, 0, unroll=2)
    lax.fori_loop(planes - 1, planes - 1, first_step, 0, unroll=2)
    lax.fori_loop(1, planes // 2 - 1, second_step, 0, unroll=2)

    def resample(phase, blocks):
        size = SHEET * rows
        pieces = half // LANE
        for b in blocks:
            spots = slice(b * size, (b + 1) * size)
            piece = jnp.concatenate(
                [scalars[phase, spots, c * LANE : (c + 2) * LANE] for c in range(pieces)], axis=0
            )
            out = jnp.dot(piece, bands[b], preferred_element_type=jnp.float32)
            for k in range(views):
                for c in range(pieces):
                    samples[k, b * SHEET : (b + 1) * SHEET, :, 2 * c * LANE : 2 * (c + 1) * LANE] = out[
                        c * size : (c + 1) * size, 2 * k * LANE : 2 * (k + 1) * LANE
                    ].reshape(SHEET, rows, 2 * LANE)

    resample(0, range(1, sheets - 1))
    depth_total = float(planes * n_group)
    dim_top = 1.00001 * -math.expm1(-planes * TABLE_TOP / depth_total)
    light_top = TABLE_TOP * dim_top
    g_copies = []

    def visitor(k):
        level_of = lax.broadcasted_iota(jnp.int32, (LEVELS, LANE), 0)
        lines = []
        for which, scale in ((0, -LOG2_E / depth_total), (1, 1.0)):
            values = [table[k, which, l] * scale for l in range(LEVELS)]
            intercepts = jnp.full((LEVELS, LANE), values[LEVELS - 1], jnp.float32)
            slopes = jnp.zeros((LEVELS, LANE), jnp.float32)
            for l in range(LEVELS - 1):
                slope = values[l + 1] - values[l]
                slopes = jnp.where(level_of == l, slope, slopes)
                intercepts = jnp.where(level_of == l, values[l] - l * slope, intercepts)
            lines += [intercepts, slopes]
        ascending = order[k, 1] > order[k, 0]

        def line(which, level, q):
            picked = [
                jnp.take_along_axis(values, level, axis=0, mode="promise_in_bounds")
                for values in lines[2 * which : 2 * which + 2]
            ]
            return picked[0] + picked[1] * q

        def visit(i, state):
            p = jnp.where(ascending, i, planes - 1 - i)
            after = []
            for start, (light, depth_log, clear) in zip(starts, state):
                q = jnp.clip(samples[k, p, :, start : start + LANE], 0.0, LEVELS - 1.0)
                level = q.astype(jnp.int32)
                depth_log = depth_log + line(0, level, q)
                left = jnp.exp2(depth_log)
                after.append((light + line(1, level, q) * (clear - left), depth_log, left))
            return tuple(after)

        return visit

    starts = range(0, depth, LANE)
    none = jnp.zeros((rows, LANE), jnp.float32)
    fresh = tuple((none, none, none + 1.0) for start in starts)

    def render_inside(k):
        state = lax.fori_loop(SHEET, planes - SHEET, visitor(k), fresh, unroll=8)
        for start, (light, depth_log, _) in zip(starts, state):
            inside[k, 0, :, start : start + LANE] = light
            inside[k, 1, :, start : start + LANE] = depth_log

    def render(phase, k):
        visit = visitor(k)
        state = lax.fori_loop(0, SHEET, visit, fresh, unroll=8)
        after = []
        for start, (light, depth_log, clear) in zip(starts, state):
            light = light + clear * inside[k, 0, :, start : start + LANE]
            depth_log = depth_log + inside[k, 1, :, start : start + LANE]
            after.append((light, depth_log, jnp.exp2(depth_log)))
        state = lax.fori_loop(planes - SHEET, planes, visit, tuple(after), unroll=8)
        for start, (light, _, clear) in zip(starts, state):
            slabs[g, phase, k, :, start : start + LANE] = jnp.concatenate(
                [encode(light, light_top), encode(1.0 - clear, dim_top)], axis=0
            )
        for d in range(1, n_group):
            slot = slabs.at[g, phase, k]
            copy = remote(slot, slot, g_send.at[d - 1, phase, k], g_recv.at[d - 1, phase, k], at(dg=d))
            copy.start()
            g_copies.append(copy)

    for k in range(views):
        render_inside(k)

    for a in range(2):
        for copy in x_copies[a]:
            copy.wait_recv()
        for f in range(2):
            come = decode(x_in[a, f]).reshape(2, rows, wide)
            start = 0 if a == 0 else planes + 2
            raw[f, start : start + 2] = come

    for a, p in ((0, 1), (1, planes + 2)):
        raw_plane(p)
        first_step(0 if a == 0 else planes - 1, 0)
        for side, (y, _) in enumerate(ends):
            for f in range(2):
                mid_edge[a, side, f : f + 1] = mid[f, p - 1, y : y + 1]
    lax.fori_loop(0, 2, lambda i, carry: second_step(i * (planes // 2 - 1), carry), 0)

    def finish(phase, k):
        for d in range(1, n_group):
            slot = slabs.at[at(dg=-d)[0], phase, k]
            remote(slot, slot, g_send.at[d - 1, phase, k], g_recv.at[d - 1, phase, k], at(dg=d)).wait_recv()
        total = jnp.zeros((rows, depth), jnp.float32)
        coded = [slabs[slab, phase, k] for slab in range(n_group)]
        lights = [decode(one[:rows], light_top) for one in coded]
        clears = [1.0 - decode(one[rows:], dim_top) for one in coded]
        for slab in range(n_group):
            passed = lights[slab]
            for other in range(n_group):
                if other != slab:
                    ahead = order[k, other] < order[k, slab]
                    passed = passed * jnp.where(ahead, clears[other], 1.0)
            total = total + passed
        return total

    resample(0, (0, sheets - 1))
    for k in range(views):
        render(0, k)

    for side in range(2):
        for copy in y_copies[side]:
            copy.wait_recv()

    plane_of = lax.broadcasted_iota(jnp.int32, (planes, wide), 0)

    def along_x(x, low=None, high=None):
        low = 0.0 if low is None else jnp.broadcast_to(low, x.shape)
        high = 0.0 if high is None else jnp.broadcast_to(high, x.shape)
        before = jnp.where(plane_of == 0, low, pltpu.roll(x, 1, 0))
        after = jnp.where(plane_of == planes - 1, high, pltpu.roll(x, planes - 1, 0))
        return before + after

    def outer_row(side, f, far):
        near = [decode(halo_recv[side, h]) for h in range(2)]
        center = [outer[side, h] + SPREADS[h] * near[h] for h in range(2)]
        beyond = react(*near, *[along_x(near[f]) + inner[side, f] + along_z(near[f])] * 2)[f]
        beyond = beyond + SPREADS[f] * far
        beside = along_x(center[f], *[mid_edge[a, side, f : f + 1] for a in range(2)])
        beside = beside + beyond + second[side, f] + along_z(center[f])
        late[side, 0, f] = react(*center, beside, beside)[f]
        late[side, 1, f] = SPREADS[f] * SPREADS[f] * near[f]

    def add_corners(f):
        for side in range(2):
            for a, p in ((0, 0), (1, planes - 1)):
                late[side, 0, f, p : p + 1] = (
                    late[side, 0, f, p : p + 1] + 2.0 * SPREADS[f] * SPREADS[f] * edge[side, a, f : f + 1]
                )

    for side in range(2):
        outer_row(side, 1, decode(halo_recv[side, 2]))

    def mended(old, f, p, lanes):
        row = row_of[:, lanes]
        new = [[jnp.broadcast_to(late[side, i, f, pl.ds(p, 1), lanes], old.shape) for i in range(2)] for side in range(2)]
        added = jnp.where(row == 1, new[0][1], jnp.where(row == last - 1, new[1][1], 0.0))
        return jnp.where(row == 0, new[0][0], jnp.where(row == last, new[1][0], old + added))

    def mend_catalyst(pair):
        packed = []
        for p in (2 * pair, 2 * pair + 1):
            new_cat = mended(wide_cat[p], 1, p, slice(0, wide))
            cat_out[p] = new_cat[:, LANE:]
            packed.append(pack(new_cat, 1))
        put(1, pair, packed)

    for b in (*range(1, sheets - 1), 0, sheets - 1):
        if b == 0:
            for k in range(views):
                render_inside(k)
            for copy in corner_copies:
                copy.wait_recv()
            add_corners(1)
        for pair in range(SHEET // 2):
            mend_catalyst(b * (SHEET // 2) + pair)
        resample(1, (b,))

    for k in range(views):
        render(1, k)

    def second_rows(p, carry):
        for side, (_, beside) in enumerate(ends):
            second[side, 0, pl.ds(p, 1)] = mid[0, p + 1, beside : beside + 1]
        return carry

    lax.fori_loop(0, planes, second_rows, 0, unroll=4)

    for side in range(2):
        far_copies[side].wait_recv()
        far = decode(halo_recv[side, 3, :, LANE:wide])
        outer_row(side, 0, jnp.concatenate([jnp.zeros((planes, LANE), jnp.float32), far], axis=1))
    add_corners(0)

    def mend_substrate(p, carry):
        sub_out[p] = mended(second_of(0, p)[:, LANE:], 0, p, slice(LANE, wide))
        return carry

    lax.fori_loop(0, planes, mend_substrate, 0, unroll=2)

    middle = middle[:, :1] & (row_of[:, :depth] >= 0)
    for k in range(views):
        mid_rows, end_rows = finish(0, k), finish(1, k)
        images[k, :, :depth] = jnp.where(middle, mid_rows, end_rows)
        images[k, :, depth:] = pltpu.roll(jnp.where(middle, end_rows, mid_rows), rows // 2, 0)

    for copy in y_copies[0] + y_copies[1] + z_copies + x_copies[0] + x_copies[1]:
        copy.wait_send()
    for copy in corner_copies + far_copies + g_copies:
        copy.wait_send()


PIECES = 4


def hand_over(*refs):
    sources, targets, (sem,) = refs[:3], refs[3:6], refs[6:]
    copies = [pltpu.make_async_copy(a, b, sem.at[i]) for i, (a, b) in enumerate(zip(sources, targets))]
    for copy in copies:
        copy.start()
    for copy in copies:
        copy.wait()


def solution(mesh):
    counts = (mesh.shape["group"], mesh.shape["tile"], mesh.shape["sub"])

    def local(substrate, catalyst, shear_offsets, slab_order, transfer_table):
        planes, rows, depth = substrate.shape
        views = slab_order.shape[0]
        wide = depth + LANE
        sheets = planes // SHEET
        f32 = jnp.float32
        dma = pltpu.SemaphoreType.DMA
        smem = pl.BlockSpec(memory_space=pltpu.SMEM)
        vmem = pl.BlockSpec(memory_space=pltpu.VMEM)
        hbm = pl.BlockSpec(memory_space=pltpu.HBM)
        anywhere = pl.BlockSpec(memory_space=pl.ANY)
        results = pl.pallas_call(
            functools.partial(kernel, counts),
            out_shape=(
                pltpu.VMEM(substrate.shape, f32),
                pltpu.VMEM(substrate.shape, f32),
                pltpu.VMEM((views, rows, 2 * depth), f32),
            ),
            in_specs=[hbm, hbm, smem, smem, smem],
            out_specs=(vmem, vmem, vmem),
            scratch_shapes=[
                pltpu.VMEM((2, planes + 4, rows, wide), f32),
                pltpu.VMEM((2, planes + 2, rows, wide), f32),
                pltpu.VMEM((2, 4, planes, depth), jnp.int16),
                pltpu.VMEM((2, 4, planes, wide), jnp.int16),
                pltpu.VMEM((2, 4, planes, wide), f32),
                pltpu.VMEM((2, 2, planes, wide), f32),
                pltpu.VMEM((2, 2, planes, wide), f32),
                pltpu.VMEM((2, 2, planes, wide), f32),
                pltpu.VMEM((2, 2, 2, wide), f32),
                pltpu.VMEM((2, 2, 2, planes, wide), f32),
                pltpu.VMEM((planes, rows, wide), f32),
                pltpu.VMEM((2, planes, rows, LANE), f32),
                pltpu.VMEM((2, 2, 2 * rows, depth), jnp.int16),
                pltpu.VMEM((2, 2, 2 * rows, LANE), jnp.int16),
                pltpu.VMEM((2, 2, 2 * rows, wide), jnp.int16),
                pltpu.VMEM((2, 3, planes, LANE), jnp.int16),
                pltpu.VMEM((2, 2, 2, depth), f32),
                pltpu.VMEM((2, 2, 2, LANE), f32),
                pltpu.VMEM((2, 2, 2, wide), f32),
                pltpu.VMEM((2, planes * rows, depth // 2 + LANE), jnp.bfloat16),
                pltpu.VMEM((sheets, 2 * LANE, views * 2 * LANE), jnp.bfloat16),
                pltpu.VMEM((views, planes, rows, depth), f32),
                pltpu.VMEM((views, 2, rows, depth), f32),
                pltpu.VMEM((counts[0], 2, views, 2 * rows, depth), jnp.int16),
                dma((LOADS, 2)), dma((2,)), dma((2,)), dma((2, 2)), dma((2, 2)), dma((3, 2)), dma((3, 2)),
                dma((2, 2, 2)), dma((2, 2, 2)),
                dma((counts[0] - 1, 2, views)), dma((counts[0] - 1, 2, views)),
            ],
            compiler_params=pltpu.CompilerParams(collective_id=0, has_side_effects=True, vmem_limit_bytes=60 * 2**20),
        )(substrate, catalyst, shear_offsets, slab_order, transfer_table)
        return pl.pallas_call(
            hand_over,
            out_shape=tuple(jax.ShapeDtypeStruct(one.shape, one.dtype) for one in results),
            in_specs=[vmem] * 3,
            out_specs=(anywhere,) * 3,
            scratch_shapes=[dma((3,))],
            compiler_params=pltpu.CompilerParams(vmem_limit_bytes=4 * 2**20),
        )(*results)

    placed = (P("group", "tile", "sub"), P("group", "tile", "sub"), P(), P(), P())
    return jax.shard_map(
        local,
        mesh=mesh,
        in_specs=placed,
        out_specs=(P("group", "tile", "sub"), P("group", "tile", "sub"), P(None, "tile", "sub")),
        check_vma=False,
    )
```

```python
import functools
import math

import jax
import jax.numpy as jnp
from jax import lax
from jax.experimental import pallas as pl
from jax.experimental.pallas import tpu as pltpu
from jax.sharding import PartitionSpec as P

LEVELS = 8
SHEET = 8
LANE = 128
SEAM = 32
PACK = 16
LOADS = 2

SPREAD_FAST = 0.16
SPREAD_SLOW = 0.08
FEED_RATE = 0.04
KILL_RATE = 0.06
TIME_STEP = 1.0

LOG2_E = math.log2(math.e)

CODE_TOP = 65535.0
TABLE_TOP = 3.5
CODE_SHIFT = 32768.0

MESH = pl.DeviceIdType.MESH


def encode(x, bound=1.0):
    return (jnp.round(x * (CODE_TOP / bound)) - CODE_SHIFT).astype(jnp.int32).astype(jnp.int16)


def decode(x, bound=1.0):
    return (x.astype(jnp.int32).astype(jnp.float32) + CODE_SHIFT) * (bound / CODE_TOP)


SPREADS = (TIME_STEP * SPREAD_FAST, TIME_STEP * SPREAD_SLOW)
KEEP_SUB = 1.0 - TIME_STEP * (6.0 * SPREAD_FAST + FEED_RATE)
KEEP_CAT = 1.0 - TIME_STEP * (6.0 * SPREAD_SLOW + FEED_RATE + KILL_RATE)


def react(sub, cat, beside_sub, beside_cat):
    reacting = TIME_STEP * (sub * cat * cat)
    new_sub = (SPREADS[0] * beside_sub + (TIME_STEP * FEED_RATE + KEEP_SUB * sub)) - reacting
    new_cat = (SPREADS[1] * beside_cat + KEEP_CAT * cat) + reacting
    return new_sub, new_cat


def kernel(
    counts,
    sub_in, cat_in, offsets, order, table,
    sub_out, cat_out, images,
    raw, mid, halo_send, halo_recv, halo, inner, outer, second, mid_edge, late, wide_cat,
    z_out, x_out, x_ring, x_in, y_ring, rim_out, rim_ring, edge, scalars, bands, samples, inside, slabs,
    load_sem, z_send, z_recv, x_send, x_recv, y_send, y_recv, c_send, c_recv, g_send, g_recv,
):
    n_group, n_tile, n_sub = counts
    planes, rows, depth = sub_in.shape
    wide = depth + LANE
    own = pl.ds(LANE, depth)
    views = order.shape[0]
    sheets = planes // SHEET
    half = depth // 2
    last = rows - 1
    g, t, s = lax.axis_index("group"), lax.axis_index("tile"), lax.axis_index("sub")

    def at(dg=0, dt=0, ds=0):
        return (
            lax.rem(g + (dg + n_group), n_group),
            lax.rem(t + (dt + n_tile), n_tile),
            lax.rem(s + (ds + n_sub), n_sub),
        )

    partner = at(ds=1)

    barrier = pltpu.get_barrier_semaphore()
    peers = [partner]
    peers += [at(dt=b, ds=c) for b in (-1, 1) for c in (0, 1)]
    peers += [at(dg=a, dt=b, ds=c) for a in (-1, 1) for b in (-1, 1) for c in (0, 1)]
    peers += [at(dg=a, ds=1) for a in (-1, 1)]
    peers += [at(dg=d) for d in range(1, n_group)]
    for peer in peers:
        pl.semaphore_signal(barrier, inc=1, device_id=peer, device_id_type=MESH)

    inputs = (sub_in, cat_in)
    pieces = math.gcd(planes // PACK, LOADS)
    piece = planes // pieces
    loads = [
        [
            pltpu.make_async_copy(
                inputs[f].at[pl.ds(i * piece, piece)], raw.at[f, pl.ds(2 + i * piece, piece), :, own], load_sem.at[i, f]
            )
            for f in range(2)
        ]
        for i in range(pieces)
    ]
    for load in sum(loads, []):
        load.start()

    def ring_block(low, high, lane_of):
        return jnp.where(lane_of < SEAM, low, high)

    lane_of = lax.broadcasted_iota(jnp.int32, (rows, LANE), 1)
    lane_of_planes = lax.broadcasted_iota(jnp.int32, (planes, LANE), 1)
    row_of = lax.broadcasted_iota(jnp.int32, (rows, wide), 0)
    first_block, last_block = slice(LANE, 2 * LANE), slice(depth, depth + LANE)
    ends = ((0, 1), (last, last - 1))

    def band_step(index, carry):
        k = index // sheets
        b = lax.rem(index, sheets)
        shift = offsets[k, g * sheets + b]
        depth_at = lax.broadcasted_iota(jnp.int32, (2 * LANE, 2 * LANE), 0)
        column = lax.broadcasted_iota(jnp.int32, (2 * LANE, 2 * LANE), 1)
        distance = (2 * depth_at - column) + (shift - LANE)
        weight = (LEVELS - 1) * jnp.maximum(0.0, 1.0 - 0.5 * jnp.abs(distance).astype(jnp.float32))
        column_at = pl.multiple_of(k * 2 * LANE, 2 * LANE)
        bands[b, :, pl.ds(column_at, 2 * LANE)] = weight.astype(jnp.bfloat16)
        return carry

    lax.fori_loop(0, views * sheets, band_step, 0)

    def collect(p, carry):
        for side in range(2):
            near, far = ends[1 - side]
            for layer, (f, y) in enumerate(((0, near), (1, near), (1, far), (0, far))):
                halo[side, layer, pl.ds(p, 1), own] = raw[f, p + 2, y : y + 1, LANE:wide]
        return carry

    for i in range(pieces):
        for load in loads[i]:
            load.wait()
        lax.fori_loop(i * piece, (i + 1) * piece, collect, 0, unroll=4)
        here = slice(i * piece, (i + 1) * piece)
        for side in range(2):
            for layer in range(4):
                halo_send[side, layer, here] = encode(halo[side, layer, here, LANE:wide])
                if layer < 3:
                    y_ring[side, layer, here] = encode(ring_block(
                        halo[side, layer, here, first_block], halo[side, layer, here, last_block],
                        lane_of_planes[here],
                    ))

    def ring_of(f, p):
        return ring_block(raw[f, p + 2, :, first_block], raw[f, p + 2, :, last_block], lane_of)

    for a, p in ((0, planes - 1), (1, 0)):
        for f in range(2):
            around = ring_of(f, p)
            for b in range(2):
                y, _ = ends[1 - b]
                rim_out[a, b, f : f + 1] = raw[f, p + 2, y : y + 1, LANE:wide]
                rim_ring[a, b, f : f + 1] = around[y : y + 1]

    def ring_step(p, carry):
        for f in range(2):
            z_out[f, p] = ring_of(f, p)
        return carry

    lax.fori_loop(0, planes, ring_step, 0, unroll=4)
    for a in range(2):
        for f in range(2):
            here = slice(planes, planes + 2) if a == 0 else slice(2, 4)
            whole = raw[f, here, :, LANE:wide].reshape(2 * rows, depth)
            x_out[a, f] = encode(whole)
            x_ring[a, f] = encode(z_out[f, here.start - 2 : here.stop - 2].reshape(2 * rows, LANE))

    pl.semaphore_wait(barrier, len(peers))

    def remote(src, dst, send, recv, to):
        return pltpu.make_async_remote_copy(
            src_ref=src, dst_ref=dst, send_sem=send, recv_sem=recv,
            device_id=to, device_id_type=MESH,
        )

    ring = pl.ds(0, LANE)
    y_copies = [
        [
            remote(halo_send.at[side, pl.ds(0, 3)], halo_recv.at[side, pl.ds(0, 3), :, own],
                   y_send.at[0, side], y_recv.at[0, side], at(dt=1 if side == 0 else -1)),
            remote(y_ring.at[side], halo_recv.at[side, pl.ds(0, 3), :, ring],
                   y_send.at[1, side], y_recv.at[1, side], at(dt=1 if side == 0 else -1, ds=1)),
        ]
        for side in range(2)
    ]
    far_copies = [
        remote(halo_send.at[side, 3], halo_recv.at[side, 3, :, own],
               y_send.at[2, side], y_recv.at[2, side], at(dt=1 if side == 0 else -1))
        for side in range(2)
    ]
    x_copies = [
        [
            remote(x_out.at[a], x_in.at[a, :, :, own], x_send.at[0, a], x_recv.at[0, a], at(dg=1 if a == 0 else -1)),
            remote(x_ring.at[a], x_in.at[a, :, :, ring], x_send.at[1, a], x_recv.at[1, a],
                   at(dg=1 if a == 0 else -1, ds=1)),
        ]
        for a in range(2)
    ]
    z_copies = [
        [
            remote(z_out.at[f, pl.ds(start, planes // 2)], raw.at[f, pl.ds(2 + start, planes // 2), :, ring],
                   z_send.at[i, f], z_recv.at[i, f], partner)
            for f in range(2)
        ]
        for i, start in enumerate((0, planes // 2))
    ]
    corner_copies = []
    for a in range(2):
        for b in range(2):
            dg, dt = 1 if a == 0 else -1, 1 if b == 0 else -1
            corner_copies += [
                remote(rim_out.at[a, b], edge.at[b, a, :, own], c_send.at[0, a, b], c_recv.at[0, a, b], at(dg=dg, dt=dt)),
                remote(rim_ring.at[a, b], edge.at[b, a, :, ring], c_send.at[1, a, b], c_recv.at[1, a, b],
                       at(dg=dg, dt=dt, ds=1)),
            ]
    for copy in z_copies[0] + z_copies[1]:
        copy.start()
    for copy in corner_copies:
        copy.start()
    for copy in y_copies[0] + y_copies[1]:
        copy.start()
    for copy in x_copies[0] + x_copies[1]:
        copy.start()
    for copy in far_copies:
        copy.start()


    def along_z(x):
        return pltpu.roll(x, 1, 1) + pltpu.roll(x, wide - 1, 1)

    def along_y(x):
        below = jnp.where(row_of == 0, 0.0, pltpu.roll(x, 1, 0))
        above = jnp.where(row_of == last, 0.0, pltpu.roll(x, last, 0))
        return below + above

    def step(field, p):
        centers = [field[f, p] for f in range(2)]
        besides = [
            field[f, p + 1] + field[f, p - 1] + along_y(centers[f]) + along_z(centers[f]) for f in range(2)
        ]
        return react(centers[0], centers[1], besides[0], besides[1])

    def raw_plane(p):
        new = step(raw, p)
        for f in range(2):
            mid[f, p - 1] = new[f]

    def first_step(p, carry):
        raw_plane(p + 2)
        for side, (y, beside) in enumerate(ends):
            for f in range(2):
                inner[side, f, pl.ds(p, 1)] = raw[f, p + 2, y : y + 1]
                outer[side, f, pl.ds(p, 1)] = mid[f, p + 1, y : y + 1]
            second[side, 1, pl.ds(p, 1)] = mid[1, p + 1, beside : beside + 1]
        return carry

    middle = (row_of[:, : half + LANE] >= rows // 4) & (row_of[:, : half + LANE] < rows - rows // 4)
    kept = jnp.where(lane_of < SEAM, jnp.where(s == n_sub - 1, 0.0, 1.0), jnp.where(s == 0, 0.0, 1.0)) > 0.5

    def pack(cat, phase):
        cat = jnp.concatenate([jnp.where(kept, cat[:, :LANE], 0.0), cat[:, LANE:]], axis=1)
        cat = pltpu.roll(cat, wide - LANE // 2, 1)
        lower, upper = cat[:, : half + LANE], pltpu.roll(cat[:, half:], rows // 2, 0)
        return jnp.where(middle, lower, upper) if phase == 0 else jnp.where(middle, upper, lower)

    def put(phase, pair, packed):
        both = jnp.concatenate(packed, axis=0).astype(jnp.bfloat16)
        start = pair * 2 * rows if phase else pl.multiple_of(pair * 2 * rows, 2 * rows)
        scalars[phase, pl.ds(start, 2 * rows)] = both

    def second_of(f, p):
        centers = [mid[h, p + 1] for h in range(2)]
        beside = mid[f, p + 2] + mid[f, p] + along_y(centers[f]) + along_z(centers[f])
        return react(*centers, beside, beside)[f]

    def second_step(pair, carry):
        packed = []
        for p in (2 * pair, 2 * pair + 1):
            new_cat = second_of(1, p)
            cat_out[p] = new_cat[:, LANE:]
            wide_cat[p] = new_cat
            packed.append(pack(new_cat, 0))
        put(0, pair, packed)
        return carry

    for copy in z_copies[0]:
        copy.wait_recv()
    lax.fori_loop(1, planes // 2 - 1, first_step, 0, unroll=2)
    for copy in z_copies[1]:
        copy.wait_recv()
    lax.fori_loop(planes // 2 - 1, planes - 1, first_step, 0, unroll=2)
    lax.fori_loop(planes - 1, planes - 1, first_step, 0, unroll=2)
    lax.fori_loop(1, planes // 2 - 1, second_step, 0, unroll=2)

    def resample(phase, blocks):
        size = SHEET * rows
        pieces = half // LANE
        for b in blocks:
            spots = slice(b * size, (b + 1) * size)
            piece = jnp.concatenate(
                [scalars[phase, spots, c * LANE : (c + 2) * LANE] for c in range(pieces)], axis=0
            )
            out = jnp.dot(piece, bands[b], preferred_element_type=jnp.float32)
            for k in range(views):
                for c in range(pieces):
                    samples[k, b * SHEET : (b + 1) * SHEET, :, 2 * c * LANE : 2 * (c + 1) * LANE] = out[
                        c * size : (c + 1) * size, 2 * k * LANE : 2 * (k + 1) * LANE
                    ].reshape(SHEET, rows, 2 * LANE)

    resample(0, range(1, sheets - 1))
    depth_total = float(planes * n_group)
    dim_top = 1.00001 * -math.expm1(-planes * TABLE_TOP / depth_total)
    light_top = TABLE_TOP * dim_top
    g_copies = []

    def visitor(k):
        level_of = lax.broadcasted_iota(jnp.int32, (LEVELS, LANE), 0)
        lines = []
        for which, scale in ((0, -LOG2_E / depth_total), (1, 1.0)):
            values = [table[k, which, l] * scale for l in range(LEVELS)]
            intercepts = jnp.full((LEVELS, LANE), values[LEVELS - 1], jnp.float32)
            slopes = jnp.zeros((LEVELS, LANE), jnp.float32)
            for l in range(LEVELS - 1):
                slope = values[l + 1] - values[l]
                slopes = jnp.where(level_of == l, slope, slopes)
                intercepts = jnp.where(level_of == l, values[l] - l * slope, intercepts)
            lines += [intercepts, slopes]
        ascending = order[k, 1] > order[k, 0]

        def line(which, level, q):
            picked = [
                jnp.take_along_axis(values, level, axis=0, mode="promise_in_bounds")
                for values in lines[2 * which : 2 * which + 2]
            ]
            return picked[0] + picked[1] * q

        def visit(i, state):
            p = jnp.where(ascending, i, planes - 1 - i)
            after = []
            for start, (light, depth_log, clear) in zip(starts, state):
                q = jnp.clip(samples[k, p, :, start : start + LANE], 0.0, LEVELS - 1.0)
                level = q.astype(jnp.int32)
                depth_log = depth_log + line(0, level, q)
                left = jnp.exp2(depth_log)
                after.append((light + line(1, level, q) * (clear - left), depth_log, left))
            return tuple(after)

        return visit

    starts = range(0, depth, LANE)
    none = jnp.zeros((rows, LANE), jnp.float32)
    fresh = tuple((none, none, none + 1.0) for start in starts)

    def render_inside(k):
        state = lax.fori_loop(SHEET, planes - SHEET, visitor(k), fresh, unroll=8)
        for start, (light, depth_log, _) in zip(starts, state):
            inside[k, 0, :, start : start + LANE] = light
            inside[k, 1, :, start : start + LANE] = depth_log

    def render(phase, k):
        visit = visitor(k)
        state = lax.fori_loop(0, SHEET, visit, fresh, unroll=8)
        after = []
        for start, (light, depth_log, clear) in zip(starts, state):
            light = light + clear * inside[k, 0, :, start : start + LANE]
            depth_log = depth_log + inside[k, 1, :, start : start + LANE]
            after.append((light, depth_log, jnp.exp2(depth_log)))
        state = lax.fori_loop(planes - SHEET, planes, visit, tuple(after), unroll=8)
        for start, (light, _, clear) in zip(starts, state):
            slabs[g, phase, k, :, start : start + LANE] = jnp.concatenate(
                [encode(light, light_top), encode(1.0 - clear, dim_top)], axis=0
            )
        for d in range(1, n_group):
            slot = slabs.at[g, phase, k]
            copy = remote(slot, slot, g_send.at[d - 1, phase, k], g_recv.at[d - 1, phase, k], at(dg=d))
            copy.start()
            g_copies.append(copy)

    for k in range(views):
        render_inside(k)

    for a in range(2):
        for copy in x_copies[a]:
            copy.wait_recv()
        for f in range(2):
            come = decode(x_in[a, f]).reshape(2, rows, wide)
            start = 0 if a == 0 else planes + 2
            raw[f, start : start + 2] = come

    for a, p in ((0, 1), (1, planes + 2)):
        raw_plane(p)
        first_step(0 if a == 0 else planes - 1, 0)
        for side, (y, _) in enumerate(ends):
            for f in range(2):
                mid_edge[a, side, f : f + 1] = mid[f, p - 1, y : y + 1]
    lax.fori_loop(0, 2, lambda i, carry: second_step(i * (planes // 2 - 1), carry), 0)

    def finish(phase, k):
        for d in range(1, n_group):
            slot = slabs.at[at(dg=-d)[0], phase, k]
            remote(slot, slot, g_send.at[d - 1, phase, k], g_recv.at[d - 1, phase, k], at(dg=d)).wait_recv()
        total = jnp.zeros((rows, depth), jnp.float32)
        coded = [slabs[slab, phase, k] for slab in range(n_group)]
        lights = [decode(one[:rows], light_top) for one in coded]
        clears = [1.0 - decode(one[rows:], dim_top) for one in coded]
        for slab in range(n_group):
            passed = lights[slab]
            for other in range(n_group):
                if other != slab:
                    ahead = order[k, other] < order[k, slab]
                    passed = passed * jnp.where(ahead, clears[other], 1.0)
            total = total + passed
        return total

    resample(0, (0, sheets - 1))
    for k in range(views):
        render(0, k)

    for side in range(2):
        for copy in y_copies[side]:
            copy.wait_recv()

    plane_of = lax.broadcasted_iota(jnp.int32, (planes, wide), 0)

    def along_x(x, low=None, high=None):
        low = 0.0 if low is None else jnp.broadcast_to(low, x.shape)
        high = 0.0 if high is None else jnp.broadcast_to(high, x.shape)
        before = jnp.where(plane_of == 0, low, pltpu.roll(x, 1, 0))
        after = jnp.where(plane_of == planes - 1, high, pltpu.roll(x, planes - 1, 0))
        return before + after

    def outer_row(side, f, far):
        near = [decode(halo_recv[side, h]) for h in range(2)]
        center = [outer[side, h] + SPREADS[h] * near[h] for h in range(2)]
        beyond = react(*near, *[along_x(near[f]) + inner[side, f] + along_z(near[f])] * 2)[f]
        beyond = beyond + SPREADS[f] * far
        beside = along_x(center[f], *[mid_edge[a, side, f : f + 1] for a in range(2)])
        beside = beside + beyond + second[side, f] + along_z(center[f])
        late[side, 0, f] = react(*center, beside, beside)[f]
        late[side, 1, f] = SPREADS[f] * SPREADS[f] * near[f]

    def add_corners(f):
        for side in range(2):
            for a, p in ((0, 0), (1, planes - 1)):
                late[side, 0, f, p : p + 1] = (
                    late[side, 0, f, p : p + 1] + 2.0 * SPREADS[f] * SPREADS[f] * edge[side, a, f : f + 1]
                )

    for side in range(2):
        outer_row(side, 1, decode(halo_recv[side, 2]))

    def mended(old, f, p, lanes):
        row = row_of[:, lanes]
        new = [[jnp.broadcast_to(late[side, i, f, pl.ds(p, 1), lanes], old.shape) for i in range(2)] for side in range(2)]
        added = jnp.where(row == 1, new[0][1], jnp.where(row == last - 1, new[1][1], 0.0))
        return jnp.where(row == 0, new[0][0], jnp.where(row == last, new[1][0], old + added))

    def mend_catalyst(pair):
        packed = []
        for p in (2 * pair, 2 * pair + 1):
            new_cat = mended(wide_cat[p], 1, p, slice(0, wide))
            cat_out[p] = new_cat[:, LANE:]
            packed.append(pack(new_cat, 1))
        put(1, pair, packed)

    for b in (*range(1, sheets - 1), 0, sheets - 1):
        if b == 0:
            for k in range(views):
                render_inside(k)
            for copy in corner_copies:
                copy.wait_recv()
            add_corners(1)
        for pair in range(SHEET // 2):
            mend_catalyst(b * (SHEET // 2) + pair)
        resample(1, (b,))

    for k in range(views):
        render(1, k)

    def second_rows(p, carry):
        for side, (_, beside) in enumerate(ends):
            second[side, 0, pl.ds(p, 1)] = mid[0, p + 1, beside : beside + 1]
        return carry

    lax.fori_loop(0, planes, second_rows, 0, unroll=4)

    for side in range(2):
        far_copies[side].wait_recv()
        far = decode(halo_recv[side, 3, :, LANE:wide])
        outer_row(side, 0, jnp.concatenate([jnp.zeros((planes, LANE), jnp.float32), far], axis=1))
    add_corners(0)

    def mend_substrate(p, carry):
        sub_out[p] = mended(second_of(0, p)[:, LANE:], 0, p, slice(LANE, wide))
        return carry

    lax.fori_loop(0, planes, mend_substrate, 0, unroll=2)

    middle = middle[:, :1] & (row_of[:, :depth] >= 0)
    for k in range(views):
        mid_rows, end_rows = finish(0, k), finish(1, k)
        images[k, :, :depth] = jnp.where(middle, mid_rows, end_rows)
        images[k, :, depth:] = pltpu.roll(jnp.where(middle, end_rows, mid_rows), rows // 2, 0)

    for copy in y_copies[0] + y_copies[1] + z_copies[0] + z_copies[1] + x_copies[0] + x_copies[1]:
        copy.wait_send()
    for copy in corner_copies + far_copies + g_copies:
        copy.wait_send()


PIECES = 4


def hand_over(*refs):
    sources, targets, (sem,) = refs[:3], refs[3:6], refs[6:]
    copies = [pltpu.make_async_copy(a, b, sem.at[i]) for i, (a, b) in enumerate(zip(sources, targets))]
    for copy in copies:
        copy.start()
    for copy in copies:
        copy.wait()


def solution(mesh):
    counts = (mesh.shape["group"], mesh.shape["tile"], mesh.shape["sub"])

    def local(substrate, catalyst, shear_offsets, slab_order, transfer_table):
        planes, rows, depth = substrate.shape
        views = slab_order.shape[0]
        wide = depth + LANE
        sheets = planes // SHEET
        f32 = jnp.float32
        dma = pltpu.SemaphoreType.DMA
        smem = pl.BlockSpec(memory_space=pltpu.SMEM)
        vmem = pl.BlockSpec(memory_space=pltpu.VMEM)
        hbm = pl.BlockSpec(memory_space=pltpu.HBM)
        anywhere = pl.BlockSpec(memory_space=pl.ANY)
        results = pl.pallas_call(
            functools.partial(kernel, counts),
            out_shape=(
                pltpu.VMEM(substrate.shape, f32),
                pltpu.VMEM(substrate.shape, f32),
                pltpu.VMEM((views, rows, 2 * depth), f32),
            ),
            in_specs=[hbm, hbm, smem, smem, smem],
            out_specs=(vmem, vmem, vmem),
            scratch_shapes=[
                pltpu.VMEM((2, planes + 4, rows, wide), f32),
                pltpu.VMEM((2, planes + 2, rows, wide), f32),
                pltpu.VMEM((2, 4, planes, depth), jnp.int16),
                pltpu.VMEM((2, 4, planes, wide), jnp.int16),
                pltpu.VMEM((2, 4, planes, wide), f32),
                pltpu.VMEM((2, 2, planes, wide), f32),
                pltpu.VMEM((2, 2, planes, wide), f32),
                pltpu.VMEM((2, 2, planes, wide), f32),
                pltpu.VMEM((2, 2, 2, wide), f32),
                pltpu.VMEM((2, 2, 2, planes, wide), f32),
                pltpu.VMEM((planes, rows, wide), f32),
                pltpu.VMEM((2, planes, rows, LANE), f32),
                pltpu.VMEM((2, 2, 2 * rows, depth), jnp.int16),
                pltpu.VMEM((2, 2, 2 * rows, LANE), jnp.int16),
                pltpu.VMEM((2, 2, 2 * rows, wide), jnp.int16),
                pltpu.VMEM((2, 3, planes, LANE), jnp.int16),
                pltpu.VMEM((2, 2, 2, depth), f32),
                pltpu.VMEM((2, 2, 2, LANE), f32),
                pltpu.VMEM((2, 2, 2, wide), f32),
                pltpu.VMEM((2, planes * rows, depth // 2 + LANE), jnp.bfloat16),
                pltpu.VMEM((sheets, 2 * LANE, views * 2 * LANE), jnp.bfloat16),
                pltpu.VMEM((views, planes, rows, depth), f32),
                pltpu.VMEM((views, 2, rows, depth), f32),
                pltpu.VMEM((counts[0], 2, views, 2 * rows, depth), jnp.int16),
                dma((LOADS, 2)), dma((2, 2)), dma((2, 2)), dma((2, 2)), dma((2, 2)), dma((3, 2)), dma((3, 2)),
                dma((2, 2, 2)), dma((2, 2, 2)),
                dma((counts[0] - 1, 2, views)), dma((counts[0] - 1, 2, views)),
            ],
            compiler_params=pltpu.CompilerParams(collective_id=0, has_side_effects=True, vmem_limit_bytes=60 * 2**20),
        )(substrate, catalyst, shear_offsets, slab_order, transfer_table)
        return pl.pallas_call(
            hand_over,
            out_shape=tuple(jax.ShapeDtypeStruct(one.shape, one.dtype) for one in results),
            in_specs=[vmem] * 3,
            out_specs=(anywhere,) * 3,
            scratch_shapes=[dma((3,))],
            compiler_params=pltpu.CompilerParams(vmem_limit_bytes=4 * 2**20),
        )(*results)

    placed = (P("group", "tile", "sub"), P("group", "tile", "sub"), P(), P(), P())
    return jax.shard_map(
        local,
        mesh=mesh,
        in_specs=placed,
        out_specs=(P("group", "tile", "sub"), P("group", "tile", "sub"), P(None, "tile", "sub")),
        check_vma=False,
    )
```
